512 devices in a mesh: member: 4 (over x), gx: 16 (over z, core), gy: 8 (over y).
Axes of the slice: x: 4, y: 8, z: 8, core: 2. Of those that a mesh axis runs over, the one named last changes fastest.
Arguments:
- background: float32 [4, 16, 1024, 1024], P('member', None, 'gx', 'gy'), may hold values from -6 to 6
- mixing: float32 [4, 4], replicated, may hold values from 0.1 to 0.6
- kappa_sq: float32 [16, 1024, 1024], P(None, 'gx', 'gy'), may hold values from 0.05 to 1
- scaling: float32 [16, 1024, 1024], P(None, 'gx', 'gy'), may hold values from 0.5 to 2
- line_inverse: float32 [16, 4, 256, 256], P('gx'), may hold values from -3 to 3
- panels: float32 [16, 65536], P(None, ('gx', 'gy')), may hold values from -3 to 3
- values: float32 [4, 65536], P('member', ('gx', 'gy')), may hold values from -6 to 6
- targets: int32 [65536, 1], P(('gx', 'gy')), may hold values from 0 to 127; in each aligned block of 512 rows (0 to 511, 512 to 1023, ...) at most 8 rows name the same one
- spots: int32 [65536], P(('gx', 'gy')), may hold values from 0 to 8191
Outputs:
- posterior: float32 [4, 16, 1024, 1024], P('member', None, 'gx', 'gy')
The draws below stay inside these ranges and needn't reach their ends.
Inputs may be any that keep to these rules, and one draw needn't show every extreme that they name: `targets`: among the 512 stations of one device (aligned blocks) no tile is named more than 8 times. `spots`: a column x * 128 + y of the tile's plane.
All inputs are finite; a program needn't handle non-finite values.
Results may differ from the reference program's by a relative error of at most 0.00011.
Values sent between devices are 32-bit elements; how exact they have to be, the bound alone decides.
A program may use at most 64 MiB of HBM per device.

```python
import math
import jax
import jax.numpy as jnp
import numpy as np
from jax import lax

NZ = 16
CX = 64
CY = 128
STA_DEV = 512
MEMBERS = 4
NX = 1024
NY = 1024
LINE = 256
STATIONS = 65536
CAP = 8
N_GX = 16
N_GY = 8


def draw_line_inverse(key, part):
    first_key, second_key = jax.random.split(key, 2)
    shape = (NZ, NX // LINE, LINE, LINE)
    index = jnp.arange(LINE)
    gap = jnp.abs(index[:, None] - index[None, :]).astype(jnp.float32)
    reach = 0.375 * LINE
    envelope = jnp.exp(-gap / reach) / jnp.sqrt(jnp.float32(reach))
    noise = jnp.clip(jax.random.normal(first_key, shape, jnp.float32), -4.0, 4.0)
    diagonal = jax.random.uniform(second_key, shape[:3], jnp.float32, 0.7, 1.3)
    return noise * envelope + diagonal[..., None] * jnp.eye(LINE, dtype=jnp.float32)


def plant(values, stream_key, least, largest):
    extent = values.shape
    place = [jax.random.randint(jax.random.fold_in(stream_key, axis), (), 0, extent[axis]) for axis in range(len(extent))]
    values = values.at[tuple(place)].set(least)
    longest = extent.index(max(extent))
    place[longest] = (place[longest] + 1) % extent[longest]
    return values.at[tuple(place)].set(largest)


def block_scale(stream_key, extent, shards, smallest, top_value):
    loudness, own = 1.0, jax.random.fold_in(stream_key, 6)
    for dim, parts in shards:
        draws = jnp.exp(jax.random.uniform(jax.random.fold_in(own, dim), (parts,), jnp.float32, smallest / len(shards), top_value / len(shards)))
        loudness = loudness * jnp.repeat(draws, extent[dim] // parts).reshape([-1 if axis == dim else 1 for axis in range(len(extent))])
    return loudness


def shared_out(stream_key, own, number, rows, count, top, most, slope):
    ranking = jax.random.permutation(stream_key, count)
    packed, usual = portions_of(count, rows * top, most, slope, True), portions_of(count, rows * top, most, slope, False)
    places = jnp.arange(count)

    def named(sizes, turn):
        used = int((sizes > 0).sum())
        fixed = max(1, used // 4)
        passed = fixed + (places - fixed + turn * (used - fixed)) % max(1, count - fixed)
        return jnp.zeros((count,), jnp.int32).at[ranking[jnp.where(places < fixed, places, passed)]].set(jnp.asarray(sizes, jnp.int32))

    sizes = jnp.where(number % 4 == 0, named(packed, number // 4), named(usual, number - number // 4 - 1))
    mixed = jax.random.permutation(jax.random.fold_in(own, 3), count)
    source_of, receiver = mixed[0:count // 2 * 2:2], mixed[1:count // 2 * 2:2]
    margin = jnp.minimum(sizes[source_of] - 1, most - sizes[receiver]) // 2
    margin = jnp.where((source_of == ranking[0]) | (receiver == ranking[0]) | (sizes[receiver] == 0), 0, jnp.maximum(margin, 0))
    passed = jax.random.randint(jax.random.fold_in(own, 4), (count // 2,), 0, 1 << 20) % (margin + 1)
    sizes = sizes.at[source_of].add(-passed).at[receiver].add(passed)
    items = jnp.searchsorted(jnp.cumsum(sizes), jnp.arange(rows * top), side="right").astype(jnp.int32)
    grid = items.reshape(top, rows).T
    grid = grid[jax.random.permutation(jax.random.fold_in(own, 1), rows)]
    turn = jax.random.randint(jax.random.fold_in(own, 2), (rows, 1), 0, top)
    return jnp.take_along_axis(grid, (jnp.arange(top)[None, :] + turn) % top, axis=1)


def portions_of(count, total, most, skew, full):
    weights = [(1 << 20) // math.isqrt(grade ** skew) + 1 for grade in range(1, count + 1)]
    largest = most if full else min(most, max(-(-total // count), total * weights[0] // sum(weights)))
    least = 1 if total - largest >= count - 1 else 0
    given, spare = [largest] + [least] * (count - 1), total - largest - least * (count - 1)
    while spare > 0:
        movable = [i for i in range(1, count) if given[i] < largest] or [i for i in range(1, count) if given[i] < most]
        whole, budget = sum([weights[i] for i in movable]), spare
        for i in movable:
            addition = min(most - given[i], max(1, budget * weights[i] // whole), spare)
            given[i] = given[i] + addition
            spare = spare - addition
    return np.array(given)


def centred(key, shape, deviation, most, cuts=(), held_as=jnp.bfloat16):
    gain = block_scale(key, shape, cuts, -0.22, 0.18) if cuts else 1.0
    result = jax.random.normal(key, shape, jnp.float32) * deviation * gain
    return jnp.minimum(jnp.maximum(result, -most), most).astype(held_as)


def setup_inputs(seed: int = 0) -> dict:
    key_list = jax.random.split(jax.random.key(seed), 10)
    background = centred(key_list[0], (MEMBERS, NZ, NX, NY), 1.0, 6.0, ((0, 4), (2, 16), (3, 8)), jnp.float32)
    mixing = jnp.clip(jax.random.uniform(key_list[1], (MEMBERS, MEMBERS), jnp.float32, 0.1, 0.6), 0.1, 0.6)
    kappa_sq = jnp.clip(jnp.exp(math.log(1.0) - 2.9957323 * jax.random.uniform(key_list[2], (NZ, NX, NY), jnp.float32) ** block_scale(key_list[2], (NZ, NX, NY), ((1, 16), (2, 8)), -0.2, 0.2)), 0.05, 1.0)
    scaling = jnp.clip(jnp.exp(math.log(2.0) - 1.3862944 * jax.random.uniform(key_list[3], (NZ, NX, NY), jnp.float32) ** block_scale(key_list[3], (NZ, NX, NY), ((1, 16), (2, 8)), -0.2, 0.2)), 0.5, 2.0)
    line_inverse = draw_line_inverse(jax.random.fold_in(key_list[9], 71), 0)
    panels = centred(key_list[5], (NZ, STATIONS), 0.5, 3.0, ((1, 128),), jnp.float32)
    values = centred(key_list[6], (MEMBERS, STATIONS), 1.0, 6.0, ((0, 4), (1, 128)), jnp.float32)
    targets_keys = jax.random.split(jax.random.fold_in(key_list[7], 1), STATIONS // STA_DEV)
    targets_turns = jax.random.permutation(jax.random.fold_in(key_list[7], 3), STATIONS // STA_DEV)
    targets = jax.vmap(lambda own, number: shared_out(jax.random.fold_in(key_list[7], 2), own, number, STA_DEV, N_GX * N_GY, 1, CAP, 2))(targets_keys, targets_turns).reshape((STATIONS, 1))
    spots = plant(jax.random.randint(key_list[8], (STATIONS,), 0, CX * CY), jax.random.fold_in(key_list[8], 1), 0, (CX * CY) - 1).astype(jnp.int32)
    return dict(background=background, mixing=mixing, kappa_sq=kappa_sq, scaling=scaling, line_inverse=line_inverse, panels=panels, values=values, targets=targets, spots=spots)


def reference(background, mixing, kappa_sq, scaling, line_inverse, panels, values, targets, spots):
    highest = lax.Precision.HIGHEST
    prior = jnp.einsum('mk,kzxy->mzxy', mixing, background, precision=highest)
    tile_id = targets[:, 0]
    row_cell = (tile_id // N_GY) * CX + spots // CY
    col_cell = (tile_id % N_GY) * CY + spots % CY
    columns = (row_cell * NY + col_cell).astype(jnp.int32)

    def station_sum(weights):
        flat = jnp.zeros((MEMBERS, NZ, NX * NY), jnp.float32)
        flat = flat.at[:, :, columns].add(panels[None] * weights[:, None, :])
        return flat.reshape(MEMBERS, NZ, NX, NY)

    def observed(field):
        picked = field.reshape(MEMBERS, NZ, NX * NY)[:, :, columns]
        return station_sum(jnp.sum(panels[None] * picked, axis=1))

    def precondition(resid):
        blocks = resid.reshape(MEMBERS, NZ, NX // LINE, LINE, NY)
        solved = jnp.einsum('zbij,mzbjy->mzbiy', line_inverse, blocks, precision=highest)
        return solved.reshape(MEMBERS, NZ, NX, NY)

    def stencil(field):
        scaled = scaling[None] * field
        padded = jnp.pad(scaled, ((0, 0), (1, 1), (1, 1), (1, 1)))
        beside = padded[:, 2:, 1:-1, 1:-1] + padded[:, :-2, 1:-1, 1:-1]
        beside = beside + padded[:, 1:-1, 2:, 1:-1] + padded[:, 1:-1, :-2, 1:-1]
        beside = beside + padded[:, 1:-1, 1:-1, 2:] + padded[:, 1:-1, 1:-1, :-2]
        return kappa_sq[None] * field + scaling[None] * (6.0 * scaled - beside)

    forcing = station_sum(values)
    first = precondition(forcing - observed(prior))
    second = first + precondition(forcing - observed(prior + first) - stencil(first))
    return prior + second
```

```python
import functools

import jax
import jax.numpy as jnp
from jax import lax
from jax.experimental import pallas as pl
from jax.experimental.pallas import tpu as pltpu
from jax.sharding import PartitionSpec as P

F32 = jnp.float32
BF16 = jnp.bfloat16
VMEM = pl.BlockSpec(memory_space=pltpu.VMEM)
NT = (((1,), (1,)), ((), ()))
TN = (((0,), (0,)), ((), ()))


def halves(value):
    high = value.astype(BF16)
    return high, (value - high.astype(F32)).astype(BF16)


def place_kernel(slot_cap, owner_col, owner_row, panels, values, spots, sent):
    count = owner_col.shape[0]
    tiles = sent.shape[0]
    depth = panels.shape[0]
    own = lax.broadcasted_iota(jnp.int32, (count, tiles), 1) == owner_col[...]
    hits = jnp.where(own, 1.0, 0.0).astype(F32)
    later = lax.broadcasted_iota(jnp.int32, (count, count), 0)
    sooner = lax.broadcasted_iota(jnp.int32, (count, count), 1)
    earlier = jnp.where(later > sooner, 1.0, 0.0).astype(BF16)
    before = jnp.dot(earlier, hits.astype(BF16), preferred_element_type=F32)
    rank = jnp.sum(before * hits, axis=1, keepdims=True).astype(jnp.int32)
    mine = lax.broadcasted_iota(jnp.int32, (tiles, count), 0) == owner_row[...]
    hits_t = jnp.where(mine, 1.0, 0.0).astype(BF16)
    hits_t = jnp.concatenate([hits_t, hits_t], axis=1)
    lane = lax.broadcasted_iota(jnp.int32, (count, slot_cap * depth), 1)
    stacked = jnp.concatenate([panels[...]] * slot_cap, axis=0).T
    body = jnp.where(lane // depth == rank, stacked, 0.0)
    sent[:, : slot_cap * depth] = jnp.dot(
        hits_t, jnp.concatenate(halves(body), axis=0), preferred_element_type=F32
    )
    value_rows = jnp.broadcast_to(values[...], (slot_cap, count))
    spot_rows = jnp.broadcast_to(spots[...].astype(F32), (slot_cap, count))
    rest = jnp.zeros((slot_cap * (depth - 2), count), F32)
    stacked = jnp.concatenate([value_rows, spot_rows, rest], axis=0).T
    extra = jnp.where(lane % slot_cap == rank, stacked, 0.0)
    sent[:, slot_cap * depth :] = jnp.dot(
        hits_t, jnp.concatenate(halves(extra), axis=0), preferred_element_type=F32
    )


def masks(cells, width_x, width_y):
    count = cells.shape[1]
    at_x = lax.broadcasted_iota(jnp.int32, (width_x, count), 0) == cells // width_y
    at_y = lax.broadcasted_iota(jnp.int32, (width_y, count), 0) == cells % width_y
    return at_x, jnp.where(at_y, 1.0, 0.0).astype(BF16)


def project(field, panels, at_x, at_y):
    depth, width_x, width_y = field.shape
    count = at_y.shape[1]
    both = jnp.concatenate([at_y, at_y], axis=0)
    total = jnp.zeros((1, count), F32)
    for z in range(0, depth, 4):
        rows = field[z : z + 4].reshape(4 * width_x, width_y)
        seen = jnp.dot(
            jnp.concatenate(halves(rows), axis=1), both, preferred_element_type=F32
        ).reshape(4, width_x, count)
        seen = jnp.sum(jnp.where(at_x[None], seen, 0.0), axis=1)
        total = total + jnp.sum(seen * panels[z : z + 4], axis=0, keepdims=True)
    return total


def scattered(weights, panels, at_x, at_y, z):
    both = jnp.concatenate([at_y, at_y], axis=1)
    scaled = panels[z : z + 4] * weights
    high = scaled.astype(BF16).astype(F32)
    parts = [high, scaled - high]
    rows = [
        jnp.where(at_x[None], part[:, None, :], 0.0).reshape(4 * at_x.shape[0], -1).astype(BF16)
        for part in parts
    ]
    out = lax.dot_general(
        jnp.concatenate(rows, axis=1), both, NT, preferred_element_type=F32
    )
    return out.reshape(4, at_x.shape[0], at_y.shape[0])


def first_kernel(slot_cap, prior, got, resid, panels, weights, cells):
    depth, width_x, width_y = prior.shape
    tiles = got.shape[0]
    body = got[:, : slot_cap * depth].T
    extra = got[:, slot_cap * depth :].T
    for k in range(slot_cap):
        lanes = pl.ds(k * tiles, tiles)
        panels[:, lanes] = body[k * depth : (k + 1) * depth]
        weights[:, lanes] = extra[k : k + 1]
        cells[:, lanes] = extra[slot_cap + k : slot_cap + k + 1].astype(jnp.int32)
    at_x, at_y = masks(cells[...], width_x, width_y)
    left = weights[...] - project(prior, panels, at_x, at_y)
    weights[...] = left
    for z in range(0, depth, 4):
        resid[z : z + 4] = scattered(left, panels, at_x, at_y, z)


def second_kernel(first, kappa, scaling, x_low, x_high, y_low, y_high, panels, weights, cells, resid):
    depth, width_x, width_y = first.shape
    at_x, at_y = masks(cells[...], width_x, width_y)
    left = weights[...] - project(first, panels, at_x, at_y)
    column = lax.broadcasted_iota(jnp.int32, (width_x, width_y), 1)
    row = lax.broadcasted_iota(jnp.int32, (width_x, width_y), 0)
    low_y, high_y = y_low[...].T, y_high[...].T
    levels = [scaling[z] * first[z] for z in range(depth)]
    for z in range(0, depth, 4):
        summed = scattered(left, panels, at_x, at_y, z)
        for k in range(z, z + 4):
            here = levels[k]
            beside = jnp.where(row == 0, x_low[k : k + 1], pltpu.roll(here, 1, 0))
            beside = beside + jnp.where(
                row == width_x - 1, x_high[k : k + 1], pltpu.roll(here, width_x - 1, 0)
            )
            beside = beside + jnp.where(
                column == 0, low_y[:, k : k + 1], pltpu.roll(here, 1, 1)
            )
            beside = beside + jnp.where(
                column == width_y - 1, high_y[:, k : k + 1], pltpu.roll(here, width_y - 1, 1)
            )
            if k > 0:
                beside = beside + levels[k - 1]
            if k < depth - 1:
                beside = beside + levels[k + 1]
            resid[k] = summed[k - z] - (
                kappa[k] * first[k] + scaling[k] * (6.0 * here - beside)
            )


def shape(*dims, dtype=F32):
    return jax.ShapeDtypeStruct(dims, dtype)


def shards(background, mixing, kappa_sq, scaling, line_inverse, panels, values, targets, spots):
    depth, width_x, width_y = kappa_sq.shape
    member = lax.axis_index("member")
    picked = lax.dynamic_slice_in_dim(mixing, member, 1, 1)[:, 0]
    prior = lax.psum_scatter(
        picked[:, None, None, None] * background, "member", scatter_dimension=0, tiled=True
    )[0]
    tiles = lax.axis_size("gx") * lax.axis_size("gy")
    count = spots.shape[0]
    slot_cap = max(2, 2 * count // tiles)
    sent = pl.pallas_call(
        functools.partial(place_kernel, slot_cap),
        out_shape=shape(tiles, 2 * slot_cap * depth),
        in_specs=[VMEM] * 5,
        out_specs=VMEM,
    )(targets, targets.reshape(1, count), panels, values, spots.reshape(1, count))
    got = lax.all_to_all(sent, ("gx", "gy"), split_axis=0, concat_axis=0, tiled=True)
    slots = tiles * slot_cap
    resid, held, weights, cells = pl.pallas_call(
        functools.partial(first_kernel, slot_cap),
        out_shape=(
            shape(depth, width_x, width_y),
            shape(depth, slots),
            shape(1, slots),
            shape(1, slots, dtype=jnp.int32),
        ),
        in_specs=[VMEM] * 2,
        out_specs=[VMEM] * 4,
    )(prior, got)
    line = line_inverse.shape[2]

    def precondition(field):
        pencil = lax.all_to_all(field, "gx", split_axis=0, concat_axis=1, tiled=True)
        blocks = pencil.reshape(pencil.shape[0], -1, line, width_y)
        solved = jnp.einsum("zbij,zbjy->zbiy", line_inverse, blocks, precision=lax.Precision.HIGHEST)
        return lax.all_to_all(
            solved.reshape(pencil.shape), "gx", split_axis=1, concat_axis=0, tiled=True
        )

    first = precondition(resid)

    def neighbours(low_side, high_side, axis):
        forward = [(i, i + 1) for i in range(lax.axis_size(axis) - 1)]
        backward = [(i + 1, i) for i in range(lax.axis_size(axis) - 1)]
        return lax.ppermute(high_side, axis, forward), lax.ppermute(low_side, axis, backward)

    x_low, x_high = neighbours(scaling[:, 0] * first[:, 0], scaling[:, -1] * first[:, -1], "gx")
    y_low, y_high = neighbours(
        scaling[:, :, 0] * first[:, :, 0], scaling[:, :, -1] * first[:, :, -1], "gy"
    )
    again = pl.pallas_call(
        second_kernel,
        out_shape=shape(depth, width_x, width_y),
        in_specs=[VMEM] * 10,
        out_specs=VMEM,
    )(first, kappa_sq, scaling, x_low, x_high, y_low, y_high, held, weights, cells)
    return (prior + (first + precondition(again)))[None]


def solution(mesh):
    return jax.shard_map(
        shards,
        mesh=mesh,
        in_specs=(
            P("member", None, "gx", "gy"),
            P(),
            P(None, "gx", "gy"),
            P(None, "gx", "gy"),
            P("gx", None, None, None),
            P(None, ("gx", "gy")),
            P("member", ("gx", "gy")),
            P(("gx", "gy"), None),
            P(("gx", "gy")),
        ),
        out_specs=P("member", None, "gx", "gy"),
        check_vma=False,
    )
```

```python
import functools

import jax
import jax.numpy as jnp
from jax import lax
from jax.experimental import pallas as pl
from jax.experimental.pallas import tpu as pltpu
from jax.sharding import PartitionSpec as P

F32 = jnp.float32
BF16 = jnp.bfloat16
VMEM = pl.BlockSpec(memory_space=pltpu.VMEM)
ANY = pl.BlockSpec(memory_space=pl.ANY)
MESH = pl.DeviceIdType.MESH
NT = (((1,), (1,)), ((), ()))
TN = (((0,), (0,)), ((), ()))


def halves(value):
    high = value.astype(BF16)
    return high, (value - high.astype(F32)).astype(BF16)


def place_kernel(slot_cap, grid_y, owner_col, owner_row, panels, values, spots, sent):
    count = owner_col.shape[0]
    tiles = sent.shape[0]
    depth = panels.shape[0]
    grid_x = tiles // grid_y
    column = (owner_col[...] % grid_y) * grid_x + owner_col[...] // grid_y
    across = (owner_row[...] % grid_y) * grid_x + owner_row[...] // grid_y
    own = lax.broadcasted_iota(jnp.int32, (count, tiles), 1) == column
    hits = jnp.where(own, 1.0, 0.0).astype(F32)
    later = lax.broadcasted_iota(jnp.int32, (count, count), 0)
    sooner = lax.broadcasted_iota(jnp.int32, (count, count), 1)
    earlier = jnp.where(later > sooner, 1.0, 0.0).astype(BF16)
    before = jnp.dot(earlier, hits.astype(BF16), preferred_element_type=F32)
    rank = jnp.sum(before * hits, axis=1, keepdims=True).astype(jnp.int32)
    mine = lax.broadcasted_iota(jnp.int32, (tiles, count), 0) == across
    hits_t = jnp.where(mine, 1.0, 0.0).astype(BF16)
    hits_t = jnp.concatenate([hits_t, hits_t], axis=1)
    lane = lax.broadcasted_iota(jnp.int32, (count, slot_cap * depth), 1)
    stacked = jnp.concatenate([panels[...]] * slot_cap, axis=0).T
    body = jnp.where(lane // depth == rank, stacked, 0.0)
    sent[:, 0, :] = jnp.dot(
        hits_t, jnp.concatenate(halves(body), axis=0), preferred_element_type=F32
    )
    value_rows = jnp.broadcast_to(values[...], (slot_cap, count))
    spot_rows = jnp.broadcast_to(spots[...].astype(F32), (slot_cap, count))
    rest = jnp.zeros((slot_cap * (depth - 2), count), F32)
    stacked = jnp.concatenate([value_rows, spot_rows, rest], axis=0).T
    extra = jnp.where(lane % slot_cap == rank, stacked, 0.0)
    sent[:, 1, :] = jnp.dot(
        hits_t, jnp.concatenate(halves(extra), axis=0), preferred_element_type=F32
    )


def masks(cells, width_x, width_y):
    count = cells.shape[1]
    at_x = lax.broadcasted_iota(jnp.int32, (width_x, count), 0) == cells // width_y
    at_y = lax.broadcasted_iota(jnp.int32, (width_y, count), 0) == cells % width_y
    return at_x, jnp.where(at_y, 1.0, 0.0).astype(BF16)


def project(field, panels, at_x, at_y):
    depth, width_x, width_y = field.shape
    count = at_y.shape[1]
    both = jnp.concatenate([at_y, at_y], axis=0)
    total = jnp.zeros((1, count), F32)
    for z in range(0, depth, 4):
        rows = field[z : z + 4].reshape(4 * width_x, width_y)
        seen = jnp.dot(
            jnp.concatenate(halves(rows), axis=1), both, preferred_element_type=F32
        ).reshape(4, width_x, count)
        seen = jnp.sum(jnp.where(at_x[None], seen, 0.0), axis=1)
        total = total + jnp.sum(seen * panels[z : z + 4], axis=0, keepdims=True)
    return total


def scattered(weights, panels, at_x, at_y, z):
    both = jnp.concatenate([at_y, at_y], axis=1)
    scaled = panels[z : z + 4] * weights
    high = scaled.astype(BF16).astype(F32)
    parts = [high, scaled - high]
    rows = [
        jnp.where(at_x[None], part[:, None, :], 0.0).reshape(4 * at_x.shape[0], -1).astype(BF16)
        for part in parts
    ]
    out = lax.dot_general(
        jnp.concatenate(rows, axis=1), both, NT, preferred_element_type=F32
    )
    return out.reshape(4, at_x.shape[0], at_y.shape[0])


def greet(devices):
    barrier = pltpu.get_barrier_semaphore()
    for device in devices:
        pl.semaphore_signal(barrier, inc=1, device_id=device, device_id_type=MESH)
    pl.semaphore_wait(barrier, len(devices))


def remote(source, target, sends, receives, device):
    return pltpu.make_async_remote_copy(
        src_ref=source,
        dst_ref=target,
        send_sem=sends,
        recv_sem=receives,
        device_id=device,
        device_id_type=MESH,
    )


def spread_kernel(
    members, grid_x, grid_y, background, line, sent, others, lines, got, mid,
    own_send, own_recv, relay_send, relay_recv, line_send, line_recv, pass_send, pass_recv,
    y_send, y_recv, x_send, x_recv, here,
):
    m, g, h = lax.axis_index("member"), lax.axis_index("gx"), lax.axis_index("gy")
    right = {"member": (m + 1) % members}
    left = {"member": (m + members - 1) % members}
    along_x = [{"gx": (g + d) % grid_x} for d in range(1, grid_x)]
    along_y = [{"gy": (h + d) % grid_y} for d in range(1, grid_y)]
    mate = {"gy": h + 1 - 2 * (h % 2)}
    greet([right, left] + along_x + along_y)

    half = background.shape[0] // 2
    low, high = pl.ds(0, half), pl.ds(half, half)
    wide = lines.shape[1]
    part = wide // 2
    quads = line.shape[1] // wide
    start = pl.multiple_of((h % 2) * part, part)

    stations = [
        remote(sent.at[(h + d) % grid_y], mid.at[h], y_send.at[d - 1], y_recv.at[d - 1], along_y[d - 1])
        for d in range(1, grid_y)
    ]
    for copy in stations:
        copy.start()
    mine = pltpu.make_async_copy(sent.at[h], mid.at[h], here.at[0])
    mine.start()
    own = [
        remote(background.at[piece], others.at[slot, piece], own_send.at[k], own_recv.at[k], device)
        for k, (piece, slot, device) in enumerate(
            [(low, 0, right), (high, 1, left), (high, 0, right), (low, 1, left)]
        )
    ]
    for copy in own:
        copy.start()
    pieces = []
    for d in range(1, grid_x):
        to = (g + d) % grid_x
        rows = pl.ds(pl.multiple_of((to % quads) * wide + start, part), part)
        pieces.append(
            remote(
                line.at[to // quads, rows],
                lines.at[g, pl.ds(start, part)],
                line_send.at[d - 1],
                line_recv.at[d - 1],
                along_x[d - 1],
            )
        )
        pieces[-1].start()
    mine_rows = pl.ds(pl.multiple_of((g % quads) * wide, wide), wide)
    level = pltpu.make_async_copy(line.at[g // quads, mine_rows], lines.at[g], here.at[1])
    level.start()

    mine.wait()
    for copy in stations:
        copy.wait_recv()
    second = [
        remote(mid.at[:, (g + d) % grid_x], got.at[g], x_send.at[d - 1], x_recv.at[d - 1], along_x[d - 1])
        for d in range(1, grid_x)
    ]
    for copy in second:
        copy.start()
    last = pltpu.make_async_copy(mid.at[:, g], got.at[g], here.at[2])
    last.start()

    own[0].wait_recv()
    relay = [
        remote(others.at[0, low], others.at[2, low], relay_send.at[0], relay_recv.at[0], right),
        remote(others.at[1, high], others.at[2, high], relay_send.at[1], relay_recv.at[1], left),
    ]
    relay[0].start()
    own[1].wait_recv()
    relay[1].start()

    passed = []
    for d in range(1, grid_x):
        pieces[d - 1].wait_recv()
        came = lines.at[(g + grid_x - d) % grid_x, pl.ds(start, part)]
        passed.append(remote(came, came, pass_send.at[d - 1], pass_recv.at[d - 1], mate))
        passed[-1].start()

    level.wait()
    last.wait()
    for copy in second + passed + relay:
        copy.wait()
    for copy in own[2:]:
        copy.wait()
    for copy in own[:2] + stations + pieces:
        copy.wait_send()


def gather_kernel(field, whole, far_send, far_recv, near_send, near_recv, pass_send, pass_recv):
    g = lax.axis_index("gx")
    flip = 2 - 4 * ((g // 2) % 2)
    near = {"gx": g + 1 - 2 * (g % 2)}
    far = {"gx": g + flip}
    greet([near, far])
    chunks = far_send.shape[0]
    size = field.shape[0] // chunks
    place, other = g % 4, (g + flip) % 4
    spans = [pl.ds(c * size, size) for c in range(chunks)]
    outs, ins, passed = [], [], []
    for c, span in enumerate(spans):
        outs.append(remote(field.at[span], whole.at[place, span], far_send.at[c], far_recv.at[c], far))
        outs[-1].start()
    for c, span in enumerate(spans):
        ins.append(remote(field.at[span], whole.at[place, span], near_send.at[c], near_recv.at[c], near))
        ins[-1].start()
    for c, span in enumerate(spans):
        outs[c].wait_recv()
        passed.append(
            remote(whole.at[other, span], whole.at[other, span], pass_send.at[c], pass_recv.at[c], near)
        )
        passed[-1].start()
    for copy in ins + passed:
        copy.wait()
    for copy in outs:
        copy.wait_send()


def rim_kernel(grid_x, grid_y, x_rim, y_rim, x_low, x_high, y_low, y_high, sends, receives):
    g, h = lax.axis_index("gx"), lax.axis_index("gy")
    up_x, down_x = {"gx": (g + 1) % grid_x}, {"gx": (g + grid_x - 1) % grid_x}
    up_y, down_y = {"gy": (h + 1) % grid_y}, {"gy": (h + grid_y - 1) % grid_y}
    greet([up_x, down_x, up_y, down_y])
    copies = [
        remote(source, target, sends.at[k], receives.at[k], device)
        for k, (source, target, device) in enumerate(
            [
                (x_rim, x_low, up_x),
                (x_rim, x_high, down_x),
                (y_rim, y_low, up_y),
                (y_rim, y_high, down_y),
            ]
        )
    ]
    for copy in copies:
        copy.start()
    for copy in copies:
        copy.wait()


def first_kernel(slot_cap, members, mixing, background, others, got, prior, resid, panels, weights, cells):
    depth, width_x, width_y = background.shape
    tiles = got.shape[0]
    m = lax.axis_index("member")
    prior[...] = (
        mixing[m, m] * background[...]
        + mixing[m, (m + members - 1) % members] * others[0]
        + mixing[m, (m + 1) % members] * others[1]
        + mixing[m, (m + 2) % members] * others[2]
    )
    body = got[:, 0, :].T
    extra = got[:, 1, :].T
    for k in range(slot_cap):
        lanes = pl.ds(k * tiles, tiles)
        panels[:, lanes] = body[k * depth : (k + 1) * depth]
        weights[:, lanes] = extra[k : k + 1]
        cells[:, lanes] = extra[slot_cap + k : slot_cap + k + 1].astype(jnp.int32)
    at_x, at_y = masks(cells[...], width_x, width_y)
    left = weights[...] - project(prior, panels, at_x, at_y)
    weights[...] = left
    for z in range(0, depth, 4):
        resid[z : z + 4] = scattered(left, panels, at_x, at_y, z)


def solved_level(lines, field, whole, z):
    place = lax.axis_index("gx") % 4
    rows = jnp.concatenate(
        [jnp.where(place == p, field[z], whole[p, z]) for p in range(4)], axis=0
    )
    left = jnp.concatenate(halves(lines[z]), axis=0)
    out = jnp.dot(left, jnp.concatenate(halves(rows), axis=1), preferred_element_type=F32)
    width_x, width_y = field.shape[1:]
    return out[:width_x, :width_y] + (out[width_x:, :width_y] + out[:width_x, width_y:])


def solve_kernel(lines, field, whole, scaling, first, x_rim, y_rim):
    depth, width_x, width_y = field.shape
    lane = lax.broadcasted_iota(jnp.int32, (width_x, width_y), 1)
    rims = jnp.zeros((width_x, width_y), F32)
    for z in range(depth):
        level = solved_level(lines, field, whole, z)
        first[z] = level
        scaled = scaling[z] * level
        x_rim[z : z + 1] = scaled[:1]
        x_rim[depth + z : depth + z + 1] = scaled[width_x - 1 :]
        rims = jnp.where(lane == z, scaled[:, :1], rims)
        rims = jnp.where(lane == depth + z, scaled[:, width_y - 1 :], rims)
    y_rim[...] = rims


def finish_kernel(lines, field, whole, prior, first, out):
    for z in range(field.shape[0]):
        out[z] = prior[z] + (first[z] + solved_level(lines, field, whole, z))


def second_kernel(
    grid_x, grid_y, first, kappa, scaling, x_low, x_high, y_low, y_high, panels, weights, cells, resid
):
    depth, width_x, width_y = first.shape
    g, h = lax.axis_index("gx"), lax.axis_index("gy")
    at_x, at_y = masks(cells[...], width_x, width_y)
    left = weights[...] - project(first, panels, at_x, at_y)
    column = lax.broadcasted_iota(jnp.int32, (width_x, width_y), 1)
    row = lax.broadcasted_iota(jnp.int32, (width_x, width_y), 0)
    low_x = jnp.where(g > 0, x_low[...], 0.0)
    high_x = jnp.where(g < grid_x - 1, x_high[...], 0.0)
    low_y = jnp.where(h > 0, y_low[...], 0.0)
    high_y = jnp.where(h < grid_y - 1, y_high[...], 0.0)
    levels = [scaling[z] * first[z] for z in range(depth)]
    for z in range(0, depth, 4):
        summed = scattered(left, panels, at_x, at_y, z)
        for k in range(z, z + 4):
            here = levels[k]
            beside = jnp.where(row == 0, low_x[depth + k : depth + k + 1], pltpu.roll(here, 1, 0))
            beside = beside + jnp.where(
                row == width_x - 1, high_x[k : k + 1], pltpu.roll(here, width_x - 1, 0)
            )
            beside = beside + jnp.where(
                column == 0, low_y[:, depth + k : depth + k + 1], pltpu.roll(here, 1, 1)
            )
            beside = beside + jnp.where(
                column == width_y - 1, high_y[:, k : k + 1], pltpu.roll(here, width_y - 1, 1)
            )
            if k > 0:
                beside = beside + levels[k - 1]
            if k < depth - 1:
                beside = beside + levels[k + 1]
            resid[k] = summed[k - z] - (
                kappa[k] * first[k] + scaling[k] * (6.0 * here - beside)
            )


def shape(*dims, dtype=F32):
    return jax.ShapeDtypeStruct(dims, dtype)


def dma(count):
    return pltpu.SemaphoreType.DMA((count,))


def shards(background, mixing, kappa_sq, scaling, line_inverse, panels, values, targets, spots):
    depth, width_x, width_y = kappa_sq.shape
    members = lax.axis_size("member")
    grid_x, grid_y = lax.axis_size("gx"), lax.axis_size("gy")
    tiles = grid_x * grid_y
    count = spots.shape[0]
    slot_cap = max(2, 2 * count // tiles)
    field = shape(depth, width_x, width_y)
    line = line_inverse.shape[2]
    background, line_inverse = background[0], line_inverse[0]
    sent = pl.pallas_call(
        functools.partial(place_kernel, slot_cap, grid_y),
        out_shape=shape(tiles, 2, slot_cap * depth),
        in_specs=[VMEM] * 5,
        out_specs=VMEM,
    )(targets, targets.reshape(1, count), panels, values, spots.reshape(1, count))
    pair = (2, slot_cap * depth)
    others, lines, got = pl.pallas_call(
        functools.partial(spread_kernel, members, grid_x, grid_y),
        out_shape=(
            shape(members - 1, depth, width_x, width_y),
            shape(depth, width_x, line),
            shape(grid_x, grid_y, *pair),
        ),
        in_specs=[ANY, ANY, VMEM],
        out_specs=(ANY, ANY, VMEM),
        scratch_shapes=[
            pltpu.VMEM((grid_y, grid_x, *pair), F32),
            dma(4), dma(4), dma(2), dma(2),
            dma(grid_x - 1), dma(grid_x - 1), dma(grid_x - 1), dma(grid_x - 1),
            dma(grid_y - 1), dma(grid_y - 1), dma(grid_x - 1), dma(grid_x - 1),
            dma(3),
        ],
        compiler_params=pltpu.CompilerParams(collective_id=0, has_side_effects=True),
    )(background, line_inverse, sent.reshape(grid_y, grid_x, *pair))
    slots = tiles * slot_cap
    prior, resid, held, weights, cells = pl.pallas_call(
        functools.partial(first_kernel, slot_cap, members),
        out_shape=(
            field,
            field,
            shape(depth, slots),
            shape(1, slots),
            shape(1, slots, dtype=jnp.int32),
        ),
        in_specs=[pl.BlockSpec(memory_space=pltpu.SMEM)] + [VMEM] * 3,
        out_specs=[VMEM] * 5,
    )(mixing, background, others, got.reshape(tiles, *pair))

    def gathered(piece):
        return pl.pallas_call(
            gather_kernel,
            out_shape=shape(4, depth, width_x, width_y),
            in_specs=[ANY],
            out_specs=ANY,
            scratch_shapes=[dma(4)] * 6,
            compiler_params=pltpu.CompilerParams(collective_id=1, has_side_effects=True),
        )(piece)

    first, x_rim, y_rim = pl.pallas_call(
        solve_kernel,
        out_shape=(field, shape(2 * depth, width_y), shape(width_x, width_y)),
        in_specs=[VMEM] * 4,
        out_specs=[VMEM] * 3,
    )(lines, resid, gathered(resid), scaling)
    rims = pl.pallas_call(
        functools.partial(rim_kernel, grid_x, grid_y),
        out_shape=[shape(2 * depth, width_y)] * 2 + [shape(width_x, width_y)] * 2,
        in_specs=[VMEM] * 2,
        out_specs=[VMEM] * 4,
        scratch_shapes=[dma(4), dma(4)],
        compiler_params=pltpu.CompilerParams(collective_id=2, has_side_effects=True),
    )(x_rim, y_rim)
    again = pl.pallas_call(
        functools.partial(second_kernel, grid_x, grid_y),
        out_shape=field,
        in_specs=[VMEM] * 10,
        out_specs=VMEM,
    )(first, kappa_sq, scaling, *rims, held, weights, cells)
    out = pl.pallas_call(
        finish_kernel,
        out_shape=field,
        in_specs=[VMEM] * 5,
        out_specs=VMEM,
    )(lines, again, gathered(again), prior, first)
    return out[None]


def solution(mesh):
    return jax.shard_map(
        shards,
        mesh=mesh,
        in_specs=(
            P("member", None, "gx", "gy"),
            P(),
            P(None, "gx", "gy"),
            P(None, "gx", "gy"),
            P("gx", None, None, None),
            P(None, ("gx", "gy")),
            P("member", ("gx", "gy")),
            P(("gx", "gy"), None),
            P(("gx", "gy")),
        ),
        out_specs=P("member", None, "gx", "gy"),
        check_vma=False,
    )
```

```python
import functools

import jax
import jax.numpy as jnp
from jax import lax
from jax.experimental import pallas as pl
from jax.experimental.pallas import tpu as pltpu
from jax.sharding import PartitionSpec as P

F32 = jnp.float32
BF16 = jnp.bfloat16
VMEM = pl.BlockSpec(memory_space=pltpu.VMEM)
ANY = pl.BlockSpec(memory_space=pl.ANY)
MESH = pl.DeviceIdType.MESH
NT = (((1,), (1,)), ((), ()))
TN = (((0,), (0,)), ((), ()))


def halves(value):
    high = value.astype(BF16)
    return high, (value - high.astype(F32)).astype(BF16)


def place_kernel(slot_cap, grid_y, owner_row, panels, values, spots, sent):
    count = owner_row.shape[1]
    tiles = sent.shape[0]
    depth = panels.shape[0]
    grid_x = tiles // grid_y
    across = (owner_row[...] % grid_y) * grid_x + owner_row[...] // grid_y
    mine = lax.broadcasted_iota(jnp.int32, (tiles, count), 0) == across
    hits_t = jnp.where(mine, 1.0, 0.0).astype(F32)
    hits = hits_t.T
    later = lax.broadcasted_iota(jnp.int32, (count, count), 0)
    sooner = lax.broadcasted_iota(jnp.int32, (count, count), 1)
    earlier = jnp.where(later > sooner, 1.0, 0.0).astype(BF16)
    before = jnp.dot(earlier, hits.astype(BF16), preferred_element_type=F32)
    rank = jnp.sum(before * hits, axis=1, keepdims=True).astype(jnp.int32)
    hits_t = jnp.concatenate([hits_t, hits_t], axis=1).astype(BF16)
    lane = lax.broadcasted_iota(jnp.int32, (count, slot_cap * depth), 1)
    stacked = jnp.concatenate([panels[...]] * slot_cap, axis=0).T
    body = jnp.where(lane // depth == rank, stacked, 0.0)
    sent[:, 0, :] = jnp.dot(
        hits_t, jnp.concatenate(halves(body), axis=0), preferred_element_type=F32
    )
    value_rows = jnp.broadcast_to(values[...], (slot_cap, count))
    spot_rows = jnp.broadcast_to(spots[...].astype(F32), (slot_cap, count))
    rest = jnp.zeros((slot_cap * (depth - 2), count), F32)
    stacked = jnp.concatenate([value_rows, spot_rows, rest], axis=0).T
    extra = jnp.where(lane % slot_cap == rank, stacked, 0.0)
    sent[:, 1, :] = jnp.dot(
        hits_t, jnp.concatenate(halves(extra), axis=0), preferred_element_type=F32
    )


def masks(cells, width_x, width_y):
    count = cells.shape[1]
    at_x = lax.broadcasted_iota(jnp.int32, (width_x, count), 0) == cells // width_y
    at_y = lax.broadcasted_iota(jnp.int32, (width_y, count), 0) == cells % width_y
    return at_x, jnp.where(at_y, 1.0, 0.0).astype(BF16)


def project(field, panels, at_x, at_y):
    depth, width_x, width_y = field.shape
    count = at_y.shape[1]
    both = jnp.concatenate([at_y, at_y], axis=0)
    total = jnp.zeros((1, count), F32)
    for z in range(0, depth, 4):
        rows = field[z : z + 4].reshape(4 * width_x, width_y)
        seen = jnp.dot(
            jnp.concatenate(halves(rows), axis=1), both, preferred_element_type=F32
        ).reshape(4, width_x, count)
        seen = jnp.sum(jnp.where(at_x[None], seen, 0.0), axis=1)
        total = total + jnp.sum(seen * panels[z : z + 4], axis=0, keepdims=True)
    return total


def scattered(weights, panels, at_x, at_y, z):
    both = jnp.concatenate([at_y, at_y], axis=1)
    scaled = panels[z : z + 4] * weights
    high = scaled.astype(BF16).astype(F32)
    parts = [high, scaled - high]
    rows = [
        jnp.where(at_x[None], part[:, None, :], 0.0).reshape(4 * at_x.shape[0], -1).astype(BF16)
        for part in parts
    ]
    out = lax.dot_general(
        jnp.concatenate(rows, axis=1), both, NT, preferred_element_type=F32
    )
    return out.reshape(4, at_x.shape[0], at_y.shape[0])


def greet(devices):
    barrier = pltpu.get_barrier_semaphore()
    for device in devices:
        pl.semaphore_signal(barrier, inc=1, device_id=device, device_id_type=MESH)
    pl.semaphore_wait(barrier, len(devices))


def remote(source, target, sends, receives, device):
    return pltpu.make_async_remote_copy(
        src_ref=source,
        dst_ref=target,
        send_sem=sends,
        recv_sem=receives,
        device_id=device,
        device_id_type=MESH,
    )


def spread_kernel(
    members, grid_x, grid_y, background, line, sent, others, lines, got, mid,
    own_send, own_recv, relay_send, relay_recv, line_send, line_recv, pass_send, pass_recv,
    y_send, y_recv, x_send, x_recv, here,
):
    m, g, h = lax.axis_index("member"), lax.axis_index("gx"), lax.axis_index("gy")
    right = {"member": (m + 1) % members}
    left = {"member": (m + members - 1) % members}
    along_x = [{"gx": (g + d) % grid_x} for d in range(1, grid_x)]
    along_y = [{"gy": (h + d) % grid_y} for d in range(1, grid_y)]
    mate = {"gy": h + 1 - 2 * (h % 2)}
    greet([right, left] + along_x + along_y)

    half = background.shape[0] // 2
    low, high = pl.ds(0, half), pl.ds(half, half)
    wide = lines.shape[1]
    part = wide // 2
    quads = line.shape[1] // wide
    start = pl.multiple_of((h % 2) * part, part)

    stations = [
        remote(sent.at[(h + d) % grid_y], mid.at[h], y_send.at[d - 1], y_recv.at[d - 1], along_y[d - 1])
        for d in range(1, grid_y)
    ]
    for copy in stations:
        copy.start()
    mine = pltpu.make_async_copy(sent.at[h], mid.at[h], here.at[0])
    mine.start()
    own = [
        remote(background.at[piece], others.at[slot, piece], own_send.at[k], own_recv.at[k], device)
        for k, (piece, slot, device) in enumerate(
            [(low, 0, right), (high, 1, left), (high, 0, right), (low, 1, left)]
        )
    ]
    for copy in own:
        copy.start()
    pieces = []
    for d in range(1, grid_x):
        to = (g + d) % grid_x
        rows = pl.ds(pl.multiple_of((to % quads) * wide + start, part), part)
        pieces.append(
            remote(
                line.at[to // quads, rows],
                lines.at[g, pl.ds(start, part)],
                line_send.at[d - 1],
                line_recv.at[d - 1],
                along_x[d - 1],
            )
        )
        pieces[-1].start()
    mine_rows = pl.ds(pl.multiple_of((g % quads) * wide, wide), wide)
    level = pltpu.make_async_copy(line.at[g // quads, mine_rows], lines.at[g], here.at[1])
    level.start()

    mine.wait()
    for copy in stations:
        copy.wait_recv()
    second = [
        remote(mid.at[:, (g + d) % grid_x], got.at[g], x_send.at[d - 1], x_recv.at[d - 1], along_x[d - 1])
        for d in range(1, grid_x)
    ]
    for copy in second:
        copy.start()
    last = pltpu.make_async_copy(mid.at[:, g], got.at[g], here.at[2])
    last.start()

    own[0].wait_recv()
    relay = [
        remote(others.at[0, low], others.at[2, low], relay_send.at[0], relay_recv.at[0], right),
        remote(others.at[1, high], others.at[2, high], relay_send.at[1], relay_recv.at[1], left),
    ]
    relay[0].start()
    own[1].wait_recv()
    relay[1].start()

    passed = []
    for d in range(1, grid_x):
        pieces[d - 1].wait_recv()
        came = lines.at[(g + grid_x - d) % grid_x, pl.ds(start, part)]
        passed.append(remote(came, came, pass_send.at[d - 1], pass_recv.at[d - 1], mate))
        passed[-1].start()

    level.wait()
    last.wait()
    for copy in second + passed + relay:
        copy.wait()
    for copy in own[2:]:
        copy.wait()
    for copy in own[:2] + stations + pieces:
        copy.wait_send()


def steps_kernel(
    grid_x, grid_y, resid, panels, weights, cells, lines_in, scaling_in, kappa_in, prior_in, out,
    whole, again, first, lines, scaling, kappa, prior, x_rim, y_rim, x_low, x_high, y_low, y_high,
    far_send, far_recv, near_send, near_recv, pass_send, pass_recv, rim_send, rim_recv, here,
):
    depth, width_x, width_y = resid.shape
    g, h = lax.axis_index("gx"), lax.axis_index("gy")
    flip = 2 - 4 * ((g // 2) % 2)
    turn = 1 - 2 * (g % 2)
    place, other = g % 4, (g + flip) % 4
    near, far = {"gx": g + turn}, {"gx": g + flip}
    side = {"gx": (g - turn + grid_x) % grid_x}
    up_y, down_y = {"gy": (h + 1) % grid_y}, {"gy": (h + grid_y - 1) % grid_y}
    fetched = [
        pltpu.make_async_copy(source, target, here.at[k])
        for k, (source, target) in enumerate(
            [(lines_in, lines), (scaling_in, scaling), (kappa_in, kappa), (prior_in, prior)]
        )
    ]
    greet([near, far, side, up_y, down_y])

    size = 4
    chunks = depth // size
    spans = [pl.ds(c * size, size) for c in range(chunks)]

    def start_chunk(source, target, c, k):
        to_far = remote(source, target.at[place, spans[c]], far_send.at[k], far_recv.at[k], far)
        to_near = remote(source, target.at[place, spans[c]], near_send.at[k], near_recv.at[k], near)
        to_far.start()
        to_near.start()
        return to_far, to_near

    def solve(target, sent, base, use):
        passed = []

        def finish(c):
            sent[c][1].wait_recv()
            passed[c].wait_recv()
            for z in range(c * size, c * size + size):
                rows = jnp.concatenate([target[p, z] for p in range(4)], axis=0)
                left = jnp.concatenate(halves(lines[z]), axis=0)
                both = jnp.concatenate(halves(rows), axis=1)
                full = jnp.dot(left, both, preferred_element_type=F32)
                use(z, full[:width_x, :width_y] + (full[width_x:, :width_y] + full[:width_x, width_y:]))

        for c in range(chunks):
            sent[c][0].wait_recv()
            came = target.at[other, spans[c]]
            passed.append(remote(came, came, pass_send.at[base + c], pass_recv.at[base + c], near))
            passed[c].start()
            if c > 0:
                finish(c - 1)
        finish(chunks - 1)
        for c in range(chunks):
            sent[c][0].wait_send()
            sent[c][1].wait_send()
            passed[c].wait_send()

    sent = [start_chunk(resid.at[spans[c]], whole, c, c) for c in range(chunks)]
    mine = pltpu.make_async_copy(resid, whole.at[place], here.at[4])
    mine.start()
    for copy in fetched:
        copy.start()
    at_x, at_y = masks(cells[...], width_x, width_y)
    lane = lax.broadcasted_iota(jnp.int32, (width_x, width_y), 1)
    row = lax.broadcasted_iota(jnp.int32, (width_x, width_y), 0)
    mine.wait()
    for copy in fetched:
        copy.wait()

    rims = [jnp.zeros((width_x, width_y), F32)]

    def use_first(z, level):
        first[z] = level
        scaled = scaling[z] * level
        x_rim[z : z + 1] = scaled[:1]
        x_rim[depth + z : depth + z + 1] = scaled[width_x - 1 :]
        low = jnp.where(lane == z, scaled[:, :1], rims[0])
        rims[0] = jnp.where(lane == depth + z, scaled[:, width_y - 1 :], low)

    solve(whole, sent, 0, use_first)
    y_rim[...] = rims[0]
    edges = [
        remote(source, target, rim_send.at[k], rim_recv.at[k], device)
        for k, (source, target, device) in enumerate(
            [
                (x_rim, x_low, {"gx": (g + 1) % grid_x}),
                (x_rim, x_high, {"gx": (g + grid_x - 1) % grid_x}),
                (y_rim, y_low, up_y),
                (y_rim, y_high, down_y),
            ]
        )
    ]
    for copy in edges:
        copy.start()
    left = weights[...] - project(first, panels, at_x, at_y)
    for copy in edges:
        copy.wait()
    low_x = jnp.where(g > 0, x_low[...], 0.0)
    high_x = jnp.where(g < grid_x - 1, x_high[...], 0.0)
    low_y = jnp.where(h > 0, y_low[...], 0.0)
    high_y = jnp.where(h < grid_y - 1, y_high[...], 0.0)
    sent = []
    for c in range(chunks):
        summed = scattered(left, panels, at_x, at_y, c * size)
        for k in range(c * size, c * size + size):
            here_u = scaling[k] * first[k]
            beside = jnp.where(row == 0, low_x[depth + k : depth + k + 1], pltpu.roll(here_u, 1, 0))
            beside = beside + jnp.where(
                row == width_x - 1, high_x[k : k + 1], pltpu.roll(here_u, width_x - 1, 0)
            )
            beside = beside + jnp.where(
                lane == 0, low_y[:, depth + k : depth + k + 1], pltpu.roll(here_u, 1, 1)
            )
            beside = beside + jnp.where(
                lane == width_y - 1, high_y[:, k : k + 1], pltpu.roll(here_u, width_y - 1, 1)
            )
            if k > 0:
                beside = beside + scaling[k - 1] * first[k - 1]
            if k < depth - 1:
                beside = beside + scaling[k + 1] * first[k + 1]
            again[place, k] = summed[k - c * size] - (
                kappa[k] * first[k] + scaling[k] * (6.0 * here_u - beside)
            )
        sent.append(start_chunk(again.at[place, spans[c]], again, c, chunks + c))

    def use_second(z, level):
        out[z] = prior[z] + (first[z] + level)

    solve(again, sent, chunks, use_second)


def first_kernel(slot_cap, members, mixing, background, others, got, prior, resid, panels, weights, cells):
    depth, width_x, width_y = background.shape
    tiles = got.shape[0]
    m = lax.axis_index("member")
    prior[...] = (
        mixing[m, m] * background[...]
        + mixing[m, (m + members - 1) % members] * others[0]
        + mixing[m, (m + 1) % members] * others[1]
        + mixing[m, (m + 2) % members] * others[2]
    )
    body = got[:, 0, :].T
    extra = got[:, 1, :].T
    for k in range(slot_cap):
        lanes = pl.ds(k * tiles, tiles)
        panels[:, lanes] = body[k * depth : (k + 1) * depth]
        weights[:, lanes] = extra[k : k + 1]
        cells[:, lanes] = extra[slot_cap + k : slot_cap + k + 1].astype(jnp.int32)
    at_x, at_y = masks(cells[...], width_x, width_y)
    left = weights[...] - project(prior, panels, at_x, at_y)
    weights[...] = left
    for z in range(0, depth, 4):
        resid[z : z + 4] = scattered(left, panels, at_x, at_y, z)


def shape(*dims, dtype=F32):
    return jax.ShapeDtypeStruct(dims, dtype)


def dma(count):
    return pltpu.SemaphoreType.DMA((count,))


def shards(background, mixing, kappa_sq, scaling, line_inverse, panels, values, targets, spots):
    depth, width_x, width_y = kappa_sq.shape
    members = lax.axis_size("member")
    grid_x, grid_y = lax.axis_size("gx"), lax.axis_size("gy")
    tiles = grid_x * grid_y
    count = spots.shape[0]
    slot_cap = max(2, 2 * count // tiles)
    field = shape(depth, width_x, width_y)
    line = line_inverse.shape[2]
    background, line_inverse = background[0], line_inverse[0]
    sent = pl.pallas_call(
        functools.partial(place_kernel, slot_cap, grid_y),
        out_shape=shape(tiles, 2, slot_cap * depth),
        in_specs=[VMEM] * 4,
        out_specs=VMEM,
    )(targets.reshape(1, count), panels, values, spots.reshape(1, count))
    pair = (2, slot_cap * depth)
    others, lines, got = pl.pallas_call(
        functools.partial(spread_kernel, members, grid_x, grid_y),
        out_shape=(
            shape(members - 1, depth, width_x, width_y),
            shape(depth, width_x, line),
            shape(grid_x, grid_y, *pair),
        ),
        in_specs=[ANY, ANY, VMEM],
        out_specs=(ANY, ANY, VMEM),
        scratch_shapes=[
            pltpu.VMEM((grid_y, grid_x, *pair), F32),
            dma(4), dma(4), dma(2), dma(2),
            dma(grid_x - 1), dma(grid_x - 1), dma(grid_x - 1), dma(grid_x - 1),
            dma(grid_y - 1), dma(grid_y - 1), dma(grid_x - 1), dma(grid_x - 1),
            dma(3),
        ],
        compiler_params=pltpu.CompilerParams(collective_id=0, has_side_effects=True),
    )(background, line_inverse, sent.reshape(grid_y, grid_x, *pair))
    slots = tiles * slot_cap
    prior, resid, held, weights, cells = pl.pallas_call(
        functools.partial(first_kernel, slot_cap, members),
        out_shape=(
            field,
            field,
            shape(depth, slots),
            shape(1, slots),
            shape(1, slots, dtype=jnp.int32),
        ),
        in_specs=[pl.BlockSpec(memory_space=pltpu.SMEM)] + [VMEM] * 3,
        out_specs=[VMEM] * 5,
    )(mixing, background, others, got.reshape(tiles, *pair))

    block = pltpu.VMEM((depth, width_x, width_y), F32)
    gathered = pltpu.VMEM((4, depth, width_x, width_y), F32)
    x_edge = pltpu.VMEM((2 * depth, width_y), F32)
    y_edge = pltpu.VMEM((width_x, width_y), F32)
    out = pl.pallas_call(
        functools.partial(steps_kernel, grid_x, grid_y),
        out_shape=field,
        in_specs=[VMEM] * 4 + [ANY] * 4,
        out_specs=VMEM,
        scratch_shapes=[
            gathered, gathered, block, pltpu.VMEM((depth, width_x, line), F32), block, block, block,
            x_edge, y_edge, x_edge, x_edge, y_edge, y_edge,
            dma(8), dma(8), dma(8), dma(8), dma(8), dma(8), dma(4), dma(4), dma(5),
        ],
        compiler_params=pltpu.CompilerParams(collective_id=1, has_side_effects=True),
    )(resid, held, weights, cells, lines, scaling, kappa_sq, prior)
    return out[None]


def solution(mesh):
    return jax.shard_map(
        shards,
        mesh=mesh,
        in_specs=(
            P("member", None, "gx", "gy"),
            P(),
            P(None, "gx", "gy"),
            P(None, "gx", "gy"),
            P("gx", None, None, None),
            P(None, ("gx", "gy")),
            P("member", ("gx", "gy")),
            P(("gx", "gy"), None),
            P(("gx", "gy")),
        ),
        out_specs=P("member", None, "gx", "gy"),
        check_vma=False,
    )
```

```python
import functools

import jax
import jax.numpy as jnp
from jax import lax
from jax.experimental import pallas as pl
from jax.experimental.pallas import tpu as pltpu
from jax.sharding import PartitionSpec as P

F32 = jnp.float32
BF16 = jnp.bfloat16
VMEM = pl.BlockSpec(memory_space=pltpu.VMEM)
ANY = pl.BlockSpec(memory_space=pl.ANY)
MESH = pl.DeviceIdType.MESH
NT = (((1,), (1,)), ((), ()))
TN = (((0,), (0,)), ((), ()))


def halves(value):
    high = value.astype(BF16)
    return high, (value - high.astype(F32)).astype(BF16)


def place_kernel(slot_cap, grid_y, owner_row, panels, values, spots, sent):
    count = owner_row.shape[1]
    tiles = sent.shape[0]
    depth = panels.shape[0]
    grid_x = tiles // grid_y
    across = (owner_row[...] % grid_y) * grid_x + owner_row[...] // grid_y
    mine = lax.broadcasted_iota(jnp.int32, (tiles, count), 0) == across
    hits_t = jnp.where(mine, 1.0, 0.0).astype(F32)
    hits = hits_t.T
    later = lax.broadcasted_iota(jnp.int32, (count, count), 0)
    sooner = lax.broadcasted_iota(jnp.int32, (count, count), 1)
    earlier = jnp.where(later > sooner, 1.0, 0.0).astype(BF16)
    before = jnp.dot(earlier, hits.astype(BF16), preferred_element_type=F32)
    rank = jnp.sum(before * hits, axis=1, keepdims=True).astype(jnp.int32)
    hits_t = jnp.concatenate([hits_t, hits_t], axis=1).astype(BF16)
    lane = lax.broadcasted_iota(jnp.int32, (count, slot_cap * depth), 1)
    stacked = jnp.concatenate([panels[...]] * slot_cap, axis=0).T
    body = jnp.where(lane // depth == rank, stacked, 0.0)
    sent[:, 0, :] = jnp.dot(
        hits_t, jnp.concatenate(halves(body), axis=0), preferred_element_type=F32
    )
    value_rows = jnp.broadcast_to(values[...], (slot_cap, count))
    spot_rows = jnp.broadcast_to(spots[...].astype(F32), (slot_cap, count))
    rest = jnp.zeros((slot_cap * (depth - 2), count), F32)
    stacked = jnp.concatenate([value_rows, spot_rows, rest], axis=0).T
    extra = jnp.where(lane % slot_cap == rank, stacked, 0.0)
    sent[:, 1, :] = jnp.dot(
        hits_t, jnp.concatenate(halves(extra), axis=0), preferred_element_type=F32
    )


def masks(cells, width_x, width_y):
    count = cells.shape[1]
    at_x = lax.broadcasted_iota(jnp.int32, (width_x, count), 0) == cells // width_y
    at_y = lax.broadcasted_iota(jnp.int32, (width_y, count), 0) == cells % width_y
    return at_x, jnp.where(at_y, 1.0, 0.0).astype(BF16)


def project(field, panels, at_x, at_y):
    depth, width_x, width_y = field.shape
    count = at_y.shape[1]
    both = jnp.concatenate([at_y, at_y], axis=0)
    total = jnp.zeros((1, count), F32)
    for z in range(0, depth, 4):
        rows = field[z : z + 4].reshape(4 * width_x, width_y)
        seen = jnp.dot(
            jnp.concatenate(halves(rows), axis=1), both, preferred_element_type=F32
        ).reshape(4, width_x, count)
        seen = jnp.sum(jnp.where(at_x[None], seen, 0.0), axis=1)
        total = total + jnp.sum(seen * panels[z : z + 4], axis=0, keepdims=True)
    return total


def scattered(weights, panels, at_x, at_y, z):
    both = jnp.concatenate([at_y, at_y], axis=1)
    scaled = panels[z : z + 4] * weights
    high = scaled.astype(BF16).astype(F32)
    parts = [high, scaled - high]
    rows = [
        jnp.where(at_x[None], part[:, None, :], 0.0).reshape(4 * at_x.shape[0], -1).astype(BF16)
        for part in parts
    ]
    out = lax.dot_general(
        jnp.concatenate(rows, axis=1), both, NT, preferred_element_type=F32
    )
    return out.reshape(4, at_x.shape[0], at_y.shape[0])


def greet(devices):
    barrier = pltpu.get_barrier_semaphore()
    for device in devices:
        pl.semaphore_signal(barrier, inc=1, device_id=device, device_id_type=MESH)
    pl.semaphore_wait(barrier, len(devices))


def remote(source, target, sends, receives, device):
    return pltpu.make_async_remote_copy(
        src_ref=source,
        dst_ref=target,
        send_sem=sends,
        recv_sem=receives,
        device_id=device,
        device_id_type=MESH,
    )


def spread(
    members, grid_x, grid_y, fill, background, line, sent, others, lines, got, mid,
    own_send, own_recv, relay_send, relay_recv, line_send, line_recv, pass_send, pass_recv,
    y_send, y_recv, x_send, x_recv, here,
):
    m, g, h = lax.axis_index("member"), lax.axis_index("gx"), lax.axis_index("gy")
    right = {"member": (m + 1) % members}
    left = {"member": (m + members - 1) % members}
    along_x = [{"gx": (g + d) % grid_x} for d in range(1, grid_x)]
    along_y = [{"gy": (h + d) % grid_y} for d in range(1, grid_y)]
    mate = {"gy": h + 1 - 2 * (h % 2)}
    greet([right, left] + along_x + along_y)

    half = background.shape[0] // 2
    low, high = pl.ds(0, half), pl.ds(half, half)
    wide = lines.shape[1]
    part = wide // 2
    quads = line.shape[1] // wide
    start = pl.multiple_of((h % 2) * part, part)

    own = [
        remote(background.at[piece], others.at[slot, piece], own_send.at[k], own_recv.at[k], device)
        for k, (piece, slot, device) in enumerate(
            [(low, 0, right), (high, 1, left), (high, 0, right), (low, 1, left)]
        )
    ]
    for copy in own:
        copy.start()
    pieces = []
    for d in range(1, grid_x):
        to = (g + d) % grid_x
        rows = pl.ds(pl.multiple_of((to % quads) * wide + start, part), part)
        pieces.append(
            remote(
                line.at[to // quads, rows],
                lines.at[g, pl.ds(start, part)],
                line_send.at[d - 1],
                line_recv.at[d - 1],
                along_x[d - 1],
            )
        )
        pieces[-1].start()
    mine_rows = pl.ds(pl.multiple_of((g % quads) * wide, wide), wide)
    level = pltpu.make_async_copy(line.at[g // quads, mine_rows], lines.at[g], here.at[1])
    level.start()

    fill()
    stations = [
        remote(sent.at[pl.ds((h + d) % grid_y * grid_x, grid_x)], mid.at[h], y_send.at[d - 1], y_recv.at[d - 1], along_y[d - 1])
        for d in range(1, grid_y)
    ]
    for copy in stations:
        copy.start()
    mine = pltpu.make_async_copy(sent.at[pl.ds(h * grid_x, grid_x)], mid.at[h], here.at[0])
    mine.start()
    mine.wait()
    for copy in stations:
        copy.wait_recv()
    second = [
        remote(mid.at[:, (g + d) % grid_x], got.at[pl.ds(g * grid_y, grid_y)], x_send.at[d - 1], x_recv.at[d - 1], along_x[d - 1])
        for d in range(1, grid_x)
    ]
    for copy in second:
        copy.start()
    last = pltpu.make_async_copy(mid.at[:, g], got.at[pl.ds(g * grid_y, grid_y)], here.at[2])
    last.start()

    own[0].wait_recv()
    relay = [
        remote(others.at[0, low], others.at[2, low], relay_send.at[0], relay_recv.at[0], right),
        remote(others.at[1, high], others.at[2, high], relay_send.at[1], relay_recv.at[1], left),
    ]
    relay[0].start()
    own[1].wait_recv()
    relay[1].start()

    passed = []
    for d in range(1, grid_x):
        pieces[d - 1].wait_recv()
        came = lines.at[(g + grid_x - d) % grid_x, pl.ds(start, part)]
        passed.append(remote(came, came, pass_send.at[d - 1], pass_recv.at[d - 1], mate))
        passed[-1].start()

    level.wait()
    last.wait()
    for copy in second + passed + relay:
        copy.wait()
    for copy in own[2:]:
        copy.wait()
    for copy in own[:2] + stations + pieces:
        copy.wait_send()


def unpack(slot_cap, got, panels, weights, cells):
    depth, tiles = panels.shape[0], got.shape[0]
    body = got[:, 0, :].T
    extra = got[:, 1, :].T
    for k in range(slot_cap):
        lanes = pl.ds(k * tiles, tiles)
        panels[:, lanes] = body[k * depth : (k + 1) * depth]
        weights[:, lanes] = extra[k : k + 1]
        cells[:, lanes] = extra[slot_cap + k : slot_cap + k + 1].astype(jnp.int32)


def steps_kernel(
    members, grid_x, grid_y, slot_cap,
    mixing, owner_row, panels_in, values, spots, background, line, scaling_in, kappa_in, prior, out,
    sent_slots, mid, got, others, mine_field, panels, weights, cells,
    whole, again, first, lines, scaling, kappa, x_rim, y_rim, x_low, x_high, y_low, y_high,
    own_send, own_recv, relay_send, relay_recv, line_send, line_recv, hand_send, hand_recv,
    y_send, y_recv, x_send, x_recv, there,
    far_send, far_recv, near_send, near_recv, pass_send, pass_recv, rim_send, rim_recv, here,
):
    depth, width_x, width_y = out.shape
    m = lax.axis_index("member")
    g, h = lax.axis_index("gx"), lax.axis_index("gy")
    flip = 2 - 4 * ((g // 2) % 2)
    turn = 1 - 2 * (g % 2)
    place, other = g % 4, (g + flip) % 4
    near, far = {"gx": g + turn}, {"gx": g + flip}
    up_y, down_y = {"gy": (h + 1) % grid_y}, {"gy": (h + grid_y - 1) % grid_y}
    fetched = [
        pltpu.make_async_copy(source, target, here.at[k])
        for k, (source, target) in enumerate(
            [(background, mine_field), (scaling_in, scaling), (kappa_in, kappa)]
        )
    ]
    for copy in fetched:
        copy.start()

    def fill():
        place_kernel(slot_cap, grid_y, owner_row, panels_in, values, spots, sent_slots)

    spread(
        members, grid_x, grid_y, fill, background, line, sent_slots, others, lines, got, mid,
        own_send, own_recv, relay_send, relay_recv, line_send, line_recv, hand_send, hand_recv,
        y_send, y_recv, x_send, x_recv, there,
    )
    for copy in fetched:
        copy.wait()
    prior[...] = (
        mixing[m, m] * mine_field[...]
        + mixing[m, (m + members - 1) % members] * others[0]
        + mixing[m, (m + 1) % members] * others[1]
        + mixing[m, (m + 2) % members] * others[2]
    )
    unpack(slot_cap, got, panels, weights, cells)

    size = 4
    chunks = depth // size
    spans = [pl.ds(c * size, size) for c in range(chunks)]

    def start_chunk(source, target, c, k):
        to_far = remote(source, target.at[place, spans[c]], far_send.at[k], far_recv.at[k], far)
        to_near = remote(source, target.at[place, spans[c]], near_send.at[k], near_recv.at[k], near)
        to_far.start()
        to_near.start()
        return to_far, to_near

    def solve(target, sent, base, use):
        passed = []

        def finish(c):
            sent[c][1].wait_recv()
            passed[c].wait_recv()
            for z in range(c * size, c * size + size):
                rows = jnp.concatenate([target[p, z] for p in range(4)], axis=0)
                left = jnp.concatenate(halves(lines[z]), axis=0)
                both = jnp.concatenate(halves(rows), axis=1)
                full = jnp.dot(left, both, preferred_element_type=F32)
                use(z, full[:width_x, :width_y] + (full[width_x:, :width_y] + full[:width_x, width_y:]))

        for c in range(chunks):
            sent[c][0].wait_recv()
            came = target.at[other, spans[c]]
            passed.append(remote(came, came, pass_send.at[base + c], pass_recv.at[base + c], near))
            passed[c].start()
            if c > 0:
                finish(c - 1)
        finish(chunks - 1)
        for c in range(chunks):
            sent[c][0].wait_send()
            sent[c][1].wait_send()
            passed[c].wait_send()

    at_x, at_y = masks(cells[...], width_x, width_y)
    lane = lax.broadcasted_iota(jnp.int32, (width_x, width_y), 1)
    row = lax.broadcasted_iota(jnp.int32, (width_x, width_y), 0)
    weights[...] = weights[...] - project(prior, panels, at_x, at_y)
    sent = []
    for c in range(chunks):
        whole[place, spans[c]] = scattered(weights[...], panels, at_x, at_y, c * size)
        sent.append(start_chunk(whole.at[place, spans[c]], whole, c, c))

    rims = [jnp.zeros((width_x, width_y), F32)]

    def use_first(z, level):
        first[z] = level
        scaled = scaling[z] * level
        x_rim[z : z + 1] = scaled[:1]
        x_rim[depth + z : depth + z + 1] = scaled[width_x - 1 :]
        low = jnp.where(lane == z, scaled[:, :1], rims[0])
        rims[0] = jnp.where(lane == depth + z, scaled[:, width_y - 1 :], low)

    solve(whole, sent, 0, use_first)
    y_rim[...] = rims[0]
    edges = [
        remote(source, target, rim_send.at[k], rim_recv.at[k], device)
        for k, (source, target, device) in enumerate(
            [
                (x_rim, x_low, {"gx": (g + 1) % grid_x}),
                (x_rim, x_high, {"gx": (g + grid_x - 1) % grid_x}),
                (y_rim, y_low, up_y),
                (y_rim, y_high, down_y),
            ]
        )
    ]
    for copy in edges:
        copy.start()
    left = weights[...] - project(first, panels, at_x, at_y)
    for copy in edges:
        copy.wait()
    low_x = jnp.where(g > 0, x_low[...], 0.0)
    high_x = jnp.where(g < grid_x - 1, x_high[...], 0.0)
    low_y = jnp.where(h > 0, y_low[...], 0.0)
    high_y = jnp.where(h < grid_y - 1, y_high[...], 0.0)
    sent = []
    for c in range(chunks):
        summed = scattered(left, panels, at_x, at_y, c * size)
        for k in range(c * size, c * size + size):
            here_u = scaling[k] * first[k]
            beside = jnp.where(row == 0, low_x[depth + k : depth + k + 1], pltpu.roll(here_u, 1, 0))
            beside = beside + jnp.where(
                row == width_x - 1, high_x[k : k + 1], pltpu.roll(here_u, width_x - 1, 0)
            )
            beside = beside + jnp.where(
                lane == 0, low_y[:, depth + k : depth + k + 1], pltpu.roll(here_u, 1, 1)
            )
            beside = beside + jnp.where(
                lane == width_y - 1, high_y[:, k : k + 1], pltpu.roll(here_u, width_y - 1, 1)
            )
            if k > 0:
                beside = beside + scaling[k - 1] * first[k - 1]
            if k < depth - 1:
                beside = beside + scaling[k + 1] * first[k + 1]
            again[place, k] = summed[k - c * size] - (
                kappa[k] * first[k] + scaling[k] * (6.0 * here_u - beside)
            )
        sent.append(start_chunk(again.at[place, spans[c]], again, c, chunks + c))

    def use_second(z, level):
        out[z] = first[z] + level

    solve(again, sent, chunks, use_second)


def shape(*dims, dtype=F32):
    return jax.ShapeDtypeStruct(dims, dtype)


def dma(count):
    return pltpu.SemaphoreType.DMA((count,))


def shards(background, mixing, kappa_sq, scaling, line_inverse, panels, values, targets, spots):
    depth, width_x, width_y = kappa_sq.shape
    members = lax.axis_size("member")
    grid_x, grid_y = lax.axis_size("gx"), lax.axis_size("gy")
    tiles = grid_x * grid_y
    count = spots.shape[0]
    slot_cap = max(2, 2 * count // tiles)
    field = shape(depth, width_x, width_y)
    line = line_inverse.shape[2]
    background, line_inverse = background[0], line_inverse[0]
    slots = tiles * slot_cap
    packet = pltpu.VMEM((tiles, 2, slot_cap * depth), F32)
    block = pltpu.VMEM((depth, width_x, width_y), F32)
    gathered = pltpu.VMEM((4, depth, width_x, width_y), F32)
    x_edge = pltpu.VMEM((2 * depth, width_y), F32)
    y_edge = pltpu.VMEM((width_x, width_y), F32)
    far_x, far_y = grid_x - 1, grid_y - 1
    prior, second = pl.pallas_call(
        functools.partial(steps_kernel, members, grid_x, grid_y, slot_cap),
        out_shape=(field, field),
        in_specs=[pl.BlockSpec(memory_space=pltpu.SMEM)] + [VMEM] * 4 + [ANY] * 4,
        out_specs=(VMEM, VMEM),
        scratch_shapes=[
            packet,
            pltpu.VMEM((grid_y, grid_x, 2, slot_cap * depth), F32),
            packet,
            pltpu.VMEM((members - 1, depth, width_x, width_y), F32),
            block,
            pltpu.VMEM((depth, slots), F32),
            pltpu.VMEM((1, slots), F32),
            pltpu.VMEM((1, slots), jnp.int32),
            gathered, gathered, block, pltpu.VMEM((depth, width_x, line), F32), block, block,
            x_edge, y_edge, x_edge, x_edge, y_edge, y_edge,
            dma(4), dma(4), dma(2), dma(2), dma(far_x), dma(far_x), dma(far_x), dma(far_x),
            dma(far_y), dma(far_y), dma(far_x), dma(far_x), dma(3),
            dma(8), dma(8), dma(8), dma(8), dma(8), dma(8), dma(4), dma(4), dma(3),
        ],
        compiler_params=pltpu.CompilerParams(collective_id=0, has_side_effects=True),
    )(
        mixing, targets.reshape(1, count), panels, values, spots.reshape(1, count),
        background, line_inverse, scaling, kappa_sq,
    )
    return (prior + second)[None]


def solution(mesh):
    return jax.shard_map(
        shards,
        mesh=mesh,
        in_specs=(
            P("member", None, "gx", "gy"),
            P(),
            P(None, "gx", "gy"),
            P(None, "gx", "gy"),
            P("gx", None, None, None),
            P(None, ("gx", "gy")),
            P("member", ("gx", "gy")),
            P(("gx", "gy"), None),
            P(("gx", "gy")),
        ),
        out_specs=P("member", None, "gx", "gy"),
        check_vma=False,
    )
```

```python
import functools

import jax
import jax.numpy as jnp
from jax import lax
from jax.experimental import pallas as pl
from jax.experimental.pallas import tpu as pltpu
from jax.sharding import PartitionSpec as P

F32 = jnp.float32
BF16 = jnp.bfloat16
VMEM = pl.BlockSpec(memory_space=pltpu.VMEM)
ANY = pl.BlockSpec(memory_space=pl.ANY)
MESH = pl.DeviceIdType.MESH
NT = (((1,), (1,)), ((), ()))
TN = (((0,), (0,)), ((), ()))


def halves(value):
    high = value.astype(BF16)
    return high, (value - high.astype(F32)).astype(BF16)


def place_kernel(slot_cap, grid_y, owner_row, panels, values, spots, sent):
    count = owner_row.shape[1]
    tiles = sent.shape[0]
    depth = panels.shape[0]
    grid_x = tiles // grid_y
    across = (owner_row[...] % grid_y) * grid_x + owner_row[...] // grid_y
    mine = lax.broadcasted_iota(jnp.int32, (tiles, count), 0) == across
    hits_t = jnp.where(mine, 1.0, 0.0).astype(F32)
    hits = hits_t.T
    later = lax.broadcasted_iota(jnp.int32, (count, count), 0)
    sooner = lax.broadcasted_iota(jnp.int32, (count, count), 1)
    earlier = jnp.where(later > sooner, 1.0, 0.0).astype(BF16)
    before = jnp.dot(earlier, hits.astype(BF16), preferred_element_type=F32)
    rank = jnp.sum(before * hits, axis=1, keepdims=True).astype(jnp.int32)
    hits_t = jnp.concatenate([hits_t, hits_t], axis=1).astype(BF16)
    lane = lax.broadcasted_iota(jnp.int32, (count, slot_cap * depth), 1)
    stacked = jnp.concatenate([panels[...]] * slot_cap, axis=0).T
    body = jnp.where(lane // depth == rank, stacked, 0.0)
    sent[:, 0, :] = jnp.dot(
        hits_t, jnp.concatenate(halves(body), axis=0), preferred_element_type=F32
    )
    value_rows = jnp.broadcast_to(values[...], (slot_cap, count))
    spot_rows = jnp.broadcast_to(spots[...].astype(F32), (slot_cap, count))
    rest = jnp.zeros((slot_cap * (depth - 2), count), F32)
    stacked = jnp.concatenate([value_rows, spot_rows, rest], axis=0).T
    extra = jnp.where(lane % slot_cap == rank, stacked, 0.0)
    sent[:, 1, :] = jnp.dot(
        hits_t, jnp.concatenate(halves(extra), axis=0), preferred_element_type=F32
    )


def masks(cells, width_x, width_y):
    count = cells.shape[1]
    at_x = lax.broadcasted_iota(jnp.int32, (width_x, count), 0) == cells // width_y
    at_y = lax.broadcasted_iota(jnp.int32, (width_y, count), 0) == cells % width_y
    return at_x, jnp.where(at_y, 1.0, 0.0).astype(BF16)


def project(field, panels, at_x, at_y, z):
    depth, width_x, width_y = field.shape
    count = at_y.shape[1]
    both = jnp.concatenate([at_y, at_y], axis=0)
    rows = field[z : z + 4].reshape(4 * width_x, width_y)
    seen = jnp.dot(
        jnp.concatenate(halves(rows), axis=1), both, preferred_element_type=F32
    ).reshape(4, width_x, count)
    seen = jnp.sum(jnp.where(at_x[None], seen, 0.0), axis=1)
    return jnp.sum(seen * panels[z : z + 4], axis=0, keepdims=True)


def scattered(weights, panels, at_x, at_y, z):
    both = jnp.concatenate([at_y, at_y], axis=1)
    scaled = panels[z : z + 4] * weights
    high = scaled.astype(BF16).astype(F32)
    parts = [high, scaled - high]
    rows = [
        jnp.where(at_x[None], part[:, None, :], 0.0).reshape(4 * at_x.shape[0], -1).astype(BF16)
        for part in parts
    ]
    out = lax.dot_general(
        jnp.concatenate(rows, axis=1), both, NT, preferred_element_type=F32
    )
    return out.reshape(4, at_x.shape[0], at_y.shape[0])


def greet(devices):
    barrier = pltpu.get_barrier_semaphore()
    for device in devices:
        pl.semaphore_signal(barrier, inc=1, device_id=device, device_id_type=MESH)
    pl.semaphore_wait(barrier, len(devices))


def remote(source, target, sends, receives, device):
    return pltpu.make_async_remote_copy(
        src_ref=source,
        dst_ref=target,
        send_sem=sends,
        recv_sem=receives,
        device_id=device,
        device_id_type=MESH,
    )


def spread(
    members, grid_x, grid_y, fill, ready, use, background, line, sent, others, lines, got, mid,
    own_send, own_recv, relay_send, relay_recv, line_send, line_recv, pass_send, pass_recv,
    y_send, y_recv, x_send, x_recv, here,
):
    m, g, h = lax.axis_index("member"), lax.axis_index("gx"), lax.axis_index("gy")
    right = {"member": (m + 1) % members}
    left = {"member": (m + members - 1) % members}
    along_x = [{"gx": (g + d) % grid_x} for d in range(1, grid_x)]
    along_y = [{"gy": (h + d) % grid_y} for d in range(1, grid_y)]
    mate = {"gy": h + 1 - 2 * (h % 2)}
    greet([right, left] + along_x + along_y)

    chunks = own_send.shape[0] // 2
    size = background.shape[0] // chunks
    spans = [pl.ds(c * size, size) for c in range(chunks)]
    wide = lines.shape[1]
    part = wide // 2
    quads = line.shape[1] // wide
    start = pl.multiple_of((h % 2) * part, part)

    own = [
        remote(background.at[span], others.at[slot, span], own_send.at[2 * c + slot], own_recv.at[2 * c + slot], device)
        for c, span in enumerate(spans)
        for slot, device in ((0, right), (1, left))
    ]
    for copy in own:
        copy.start()
    pieces = []
    for d in range(1, grid_x):
        to = (g + d) % grid_x
        rows = pl.ds(pl.multiple_of((to % quads) * wide + start, part), part)
        pieces.append(
            remote(
                line.at[to // quads, rows],
                lines.at[g, pl.ds(start, part)],
                line_send.at[d - 1],
                line_recv.at[d - 1],
                along_x[d - 1],
            )
        )
        pieces[-1].start()
    mine_rows = pl.ds(pl.multiple_of((g % quads) * wide, wide), wide)
    level = pltpu.make_async_copy(line.at[g // quads, mine_rows], lines.at[g], here.at[1])
    level.start()

    fill()
    stations = [
        remote(sent.at[pl.ds((h + d) % grid_y * grid_x, grid_x)], mid.at[h], y_send.at[d - 1], y_recv.at[d - 1], along_y[d - 1])
        for d in range(1, grid_y)
    ]
    for copy in stations:
        copy.start()
    mine = pltpu.make_async_copy(sent.at[pl.ds(h * grid_x, grid_x)], mid.at[h], here.at[0])
    mine.start()
    mine.wait()
    for copy in stations:
        copy.wait_recv()
    second = [
        remote(mid.at[:, (g + d) % grid_x], got.at[pl.ds(g * grid_y, grid_y)], x_send.at[d - 1], x_recv.at[d - 1], along_x[d - 1])
        for d in range(1, grid_x)
    ]
    for copy in second:
        copy.start()
    last = pltpu.make_async_copy(mid.at[:, g], got.at[pl.ds(g * grid_y, grid_y)], here.at[2])
    last.start()

    relay = []
    rows = background.shape[1] // 2
    for c, span in enumerate(spans):
        for slot, device in ((0, right), (1, left)):
            k = 2 * c + slot
            share = pl.ds(slot * rows, rows)
            own[k].wait_recv()
            relay.append(
                remote(
                    others.at[slot, span, share],
                    others.at[2, span, share],
                    relay_send.at[k],
                    relay_recv.at[k],
                    device,
                )
            )
            relay[k].start()

    last.wait()
    for copy in second:
        copy.wait_recv()
    ready()
    passed = []
    group = -(-(grid_x - 1) // chunks)
    for c in range(chunks):
        for d in range(1 + c * group, min(1 + c * group + group, grid_x)):
            pieces[d - 1].wait_recv()
            came = lines.at[(g + grid_x - d) % grid_x, pl.ds(start, part)]
            passed.append(remote(came, came, pass_send.at[d - 1], pass_recv.at[d - 1], mate))
            passed[-1].start()
        relay[2 * c].wait_recv()
        relay[2 * c + 1].wait_recv()
        use(c)
    level.wait()
    return passed, own + relay + stations + second + pieces + passed


def unpack(slot_cap, got, panels, weights, cells):
    depth, tiles = panels.shape[0], got.shape[0]
    body = got[:, 0, :].T
    extra = got[:, 1, :].T
    for k in range(slot_cap):
        lanes = pl.ds(k * tiles, tiles)
        panels[:, lanes] = body[k * depth : (k + 1) * depth]
        weights[:, lanes] = extra[k : k + 1]
        cells[:, lanes] = extra[slot_cap + k : slot_cap + k + 1].astype(jnp.int32)


def steps_kernel(
    members, grid_x, grid_y, slot_cap,
    mixing, owner_row, panels_in, values, spots, background, line, scaling_in, kappa_in, prior, out,
    sent_slots, mid, got, others, mine_field, panels, weights, cells,
    whole, again, first, lines, scaling, kappa, x_rim, y_rim, x_low, x_high, y_low, y_high,
    own_send, own_recv, relay_send, relay_recv, line_send, line_recv, hand_send, hand_recv,
    y_send, y_recv, x_send, x_recv, there,
    far_send, far_recv, near_send, near_recv, pass_send, pass_recv, rim_send, rim_recv, here,
):
    depth, width_x, width_y = out.shape
    m = lax.axis_index("member")
    g, h = lax.axis_index("gx"), lax.axis_index("gy")
    flip = 2 - 4 * ((g // 2) % 2)
    turn = 1 - 2 * (g % 2)
    place, other = g % 4, (g + flip) % 4
    near, far = {"gx": g + turn}, {"gx": g + flip}
    up_y, down_y = {"gy": (h + 1) % grid_y}, {"gy": (h + grid_y - 1) % grid_y}
    fetched = [
        pltpu.make_async_copy(source, target, here.at[k])
        for k, (source, target) in enumerate(
            [(background, mine_field), (scaling_in, scaling), (kappa_in, kappa)]
        )
    ]
    for copy in fetched:
        copy.start()

    def fill():
        place_kernel(slot_cap, grid_y, owner_row, panels_in, values, spots, sent_slots)

    size = 4
    chunks = depth // size
    spans = [pl.ds(c * size, size) for c in range(chunks)]

    seen = []

    def ready():
        for copy in fetched:
            copy.wait()
        unpack(slot_cap, got, panels, weights, cells)
        seen.extend(masks(cells[...], width_x, width_y))

    def use_prior(c):
        z = c * size
        prior[z : z + size] = (
            mixing[m, m] * mine_field[z : z + size]
            + mixing[m, (m + members - 1) % members] * others[0, z : z + size]
            + mixing[m, (m + 1) % members] * others[1, z : z + size]
            + mixing[m, (m + 2) % members] * others[2, z : z + size]
        )
        weights[...] = weights[...] - project(prior, panels, *seen, z)

    passed, unsent = spread(
        members, grid_x, grid_y, fill, ready, use_prior, background, line, sent_slots, others, lines, got, mid,
        own_send, own_recv, relay_send, relay_recv, line_send, line_recv, hand_send, hand_recv,
        y_send, y_recv, x_send, x_recv, there,
    )
    at_x, at_y = seen

    def start_chunk(source, target, c, k):
        to_far = remote(source, target.at[place, spans[c]], far_send.at[k], far_recv.at[k], far)
        to_near = remote(source, target.at[place, spans[c]], near_send.at[k], near_recv.at[k], near)
        to_far.start()
        to_near.start()
        return to_far, to_near

    def solve(target, sent, base, use, done):
        handed = []

        def finish(c):
            sent[c][1].wait_recv()
            handed[c].wait_recv()
            for z in range(c * size, c * size + size):
                rows = jnp.concatenate([target[p, z] for p in range(4)], axis=0)
                left = jnp.concatenate(halves(lines[z]), axis=0)
                both = jnp.concatenate(halves(rows), axis=1)
                full = jnp.dot(left, both, preferred_element_type=F32)
                use(z, full[:width_x, :width_y] + (full[width_x:, :width_y] + full[:width_x, width_y:]))
            done(c)

        for c in range(chunks):
            sent[c][0].wait_recv()
            came = target.at[other, spans[c]]
            handed.append(remote(came, came, pass_send.at[base + c], pass_recv.at[base + c], near))
            handed[c].start()
            if c > 0:
                finish(c - 1)
        finish(chunks - 1)
        for c in range(chunks):
            sent[c][0].wait_send()
            sent[c][1].wait_send()
            handed[c].wait_send()

    lane = lax.broadcasted_iota(jnp.int32, (width_x, width_y), 1)
    row = lax.broadcasted_iota(jnp.int32, (width_x, width_y), 0)
    sent = []
    for c in range(chunks):
        whole[place, spans[c]] = scattered(weights[...], panels, at_x, at_y, c * size)
        sent.append(start_chunk(whole.at[place, spans[c]], whole, c, c))

    for copy in passed:
        copy.wait_recv()
    rims = [jnp.zeros((width_x, width_y), F32)]
    edges = []

    def use_first(z, level):
        c, j = z // size, z % size
        first[z] = level
        scaled = scaling[z] * level
        x_rim[c, j : j + 1] = scaled[:1]
        x_rim[c, size + j : size + j + 1] = scaled[width_x - 1 :]
        low = jnp.where(lane == j, scaled[:, :1], rims[0])
        rims[0] = jnp.where(lane == size + j, scaled[:, width_y - 1 :], low)

    def send_rims(c):
        y_rim[c] = rims[0]
        edges.append(
            [
                remote(source.at[c], target.at[c], rim_send.at[4 * c + k], rim_recv.at[4 * c + k], device)
                for k, (source, target, device) in enumerate(
                    [
                        (x_rim, x_low, {"gx": (g + 1) % grid_x}),
                        (x_rim, x_high, {"gx": (g + grid_x - 1) % grid_x}),
                        (y_rim, y_low, up_y),
                        (y_rim, y_high, down_y),
                    ]
                )
            ]
        )
        for copy in edges[c]:
            copy.start()
        weights[...] = weights[...] - project(first, panels, at_x, at_y, c * size)

    solve(whole, sent, 0, use_first, send_rims)
    left = weights[...]
    sent = []
    for c in range(chunks):
        summed = scattered(left, panels, at_x, at_y, c * size)
        for copy in edges[c]:
            copy.wait()
        low_x = jnp.where(g > 0, x_low[c], 0.0)
        high_x = jnp.where(g < grid_x - 1, x_high[c], 0.0)
        low_y = jnp.where(h > 0, y_low[c], 0.0)
        high_y = jnp.where(h < grid_y - 1, y_high[c], 0.0)
        for k in range(c * size, c * size + size):
            j = k - c * size
            here_u = scaling[k] * first[k]
            beside = jnp.where(row == 0, low_x[size + j : size + j + 1], pltpu.roll(here_u, 1, 0))
            beside = beside + jnp.where(
                row == width_x - 1, high_x[j : j + 1], pltpu.roll(here_u, width_x - 1, 0)
            )
            beside = beside + jnp.where(
                lane == 0, low_y[:, size + j : size + j + 1], pltpu.roll(here_u, 1, 1)
            )
            beside = beside + jnp.where(
                lane == width_y - 1, high_y[:, j : j + 1], pltpu.roll(here_u, width_y - 1, 1)
            )
            if k > 0:
                beside = beside + scaling[k - 1] * first[k - 1]
            if k < depth - 1:
                beside = beside + scaling[k + 1] * first[k + 1]
            again[place, k] = summed[k - c * size] - (
                kappa[k] * first[k] + scaling[k] * (6.0 * here_u - beside)
            )
        sent.append(start_chunk(again.at[place, spans[c]], again, c, chunks + c))

    def use_second(z, level):
        out[z] = first[z] + level

    solve(again, sent, chunks, use_second, lambda c: None)
    for copy in unsent:
        copy.wait_send()


def shape(*dims, dtype=F32):
    return jax.ShapeDtypeStruct(dims, dtype)


def dma(count):
    return pltpu.SemaphoreType.DMA((count,))


def shards(background, mixing, kappa_sq, scaling, line_inverse, panels, values, targets, spots):
    depth, width_x, width_y = kappa_sq.shape
    members = lax.axis_size("member")
    grid_x, grid_y = lax.axis_size("gx"), lax.axis_size("gy")
    tiles = grid_x * grid_y
    count = spots.shape[0]
    slot_cap = max(2, 2 * count // tiles)
    field = shape(depth, width_x, width_y)
    line = line_inverse.shape[2]
    background, line_inverse = background[0], line_inverse[0]
    slots = tiles * slot_cap
    packet = pltpu.VMEM((tiles, 2, slot_cap * depth), F32)
    block = pltpu.VMEM((depth, width_x, width_y), F32)
    gathered = pltpu.VMEM((4, depth, width_x, width_y), F32)
    x_edge = pltpu.VMEM((4, depth // 2, width_y), F32)
    y_edge = pltpu.VMEM((4, width_x, width_y), F32)
    far_x, far_y = grid_x - 1, grid_y - 1
    prior, second = pl.pallas_call(
        functools.partial(steps_kernel, members, grid_x, grid_y, slot_cap),
        out_shape=(field, field),
        in_specs=[pl.BlockSpec(memory_space=pltpu.SMEM)] + [VMEM] * 4 + [ANY] * 4,
        out_specs=(VMEM, VMEM),
        scratch_shapes=[
            packet,
            pltpu.VMEM((grid_y, grid_x, 2, slot_cap * depth), F32),
            packet,
            pltpu.VMEM((members - 1, depth, width_x, width_y), F32),
            block,
            pltpu.VMEM((depth, slots), F32),
            pltpu.VMEM((1, slots), F32),
            pltpu.VMEM((1, slots), jnp.int32),
            gathered, gathered, block, pltpu.VMEM((depth, width_x, line), F32), block, block,
            x_edge, y_edge, x_edge, x_edge, y_edge, y_edge,
            dma(8), dma(8), dma(8), dma(8), dma(far_x), dma(far_x), dma(far_x), dma(far_x),
            dma(far_y), dma(far_y), dma(far_x), dma(far_x), dma(3),
            dma(8), dma(8), dma(8), dma(8), dma(8), dma(8), dma(16), dma(16), dma(3),
        ],
        compiler_params=pltpu.CompilerParams(collective_id=0, has_side_effects=True),
    )(
        mixing, targets.reshape(1, count), panels, values, spots.reshape(1, count),
        background, line_inverse, scaling, kappa_sq,
    )
    return (prior + second)[None]


def solution(mesh):
    return jax.shard_map(
        shards,
        mesh=mesh,
        in_specs=(
            P("member", None, "gx", "gy"),
            P(),
            P(None, "gx", "gy"),
            P(None, "gx", "gy"),
            P("gx", None, None, None),
            P(None, ("gx", "gy")),
            P("member", ("gx", "gy")),
            P(("gx", "gy"), None),
            P(("gx", "gy")),
        ),
        out_specs=P("member", None, "gx", "gy"),
        check_vma=False,
    )
```

```python
import functools

import jax
import jax.numpy as jnp
from jax import lax
from jax.experimental import pallas as pl
from jax.experimental.pallas import tpu as pltpu
from jax.sharding import PartitionSpec as P

F32 = jnp.float32
BF16 = jnp.bfloat16
VMEM = pl.BlockSpec(memory_space=pltpu.VMEM)
ANY = pl.BlockSpec(memory_space=pl.ANY)
MESH = pl.DeviceIdType.MESH
NT = (((1,), (1,)), ((), ()))
TN = (((0,), (0,)), ((), ()))


def halves(value):
    high = value.astype(BF16)
    return high, (value - high.astype(F32)).astype(BF16)


def place_kernel(slot_cap, grid_y, owner_row, panels, values, spots, sent):
    count = owner_row.shape[1]
    tiles = sent.shape[0]
    depth = panels.shape[0]
    grid_x = tiles // grid_y
    across = (owner_row[...] % grid_y) * grid_x + owner_row[...] // grid_y
    mine = lax.broadcasted_iota(jnp.int32, (tiles, count), 0) == across
    hits_t = jnp.where(mine, 1.0, 0.0).astype(F32)
    hits = hits_t.T
    later = lax.broadcasted_iota(jnp.int32, (count, count), 0)
    sooner = lax.broadcasted_iota(jnp.int32, (count, count), 1)
    earlier = jnp.where(later > sooner, 1.0, 0.0).astype(BF16)
    before = jnp.dot(earlier, hits.astype(BF16), preferred_element_type=F32)
    rank = jnp.sum(before * hits, axis=1, keepdims=True).astype(jnp.int32)
    hits_t = jnp.concatenate([hits_t, hits_t], axis=1).astype(BF16)
    lane = lax.broadcasted_iota(jnp.int32, (count, slot_cap * depth), 1)
    stacked = jnp.concatenate([panels[...]] * slot_cap, axis=0).T
    body = jnp.where(lane // depth == rank, stacked, 0.0)
    sent[:, 0, :] = jnp.dot(
        hits_t, jnp.concatenate(halves(body), axis=0), preferred_element_type=F32
    )
    value_rows = jnp.broadcast_to(values[...], (slot_cap, count))
    spot_rows = jnp.broadcast_to(spots[...].astype(F32), (slot_cap, count))
    rest = jnp.zeros((slot_cap * (depth - 2), count), F32)
    stacked = jnp.concatenate([value_rows, spot_rows, rest], axis=0).T
    extra = jnp.where(lane % slot_cap == rank, stacked, 0.0)
    sent[:, 1, :] = jnp.dot(
        hits_t, jnp.concatenate(halves(extra), axis=0), preferred_element_type=F32
    )


def masks(cells, width_x, width_y):
    count = cells.shape[1]
    at_x = lax.broadcasted_iota(jnp.int32, (width_x, count), 0) == cells // width_y
    at_y = lax.broadcasted_iota(jnp.int32, (width_y, count), 0) == cells % width_y
    return at_x, jnp.where(at_y, 1.0, 0.0).astype(BF16)


def project(field, panels, at_x, at_y, z):
    depth, width_x, width_y = field.shape
    count = at_y.shape[1]
    both = jnp.concatenate([at_y, at_y], axis=0)
    rows = field[z : z + 4].reshape(4 * width_x, width_y)
    seen = jnp.dot(
        jnp.concatenate(halves(rows), axis=1), both, preferred_element_type=F32
    ).reshape(4, width_x, count)
    seen = jnp.sum(jnp.where(at_x[None], seen, 0.0), axis=1)
    return jnp.sum(seen * panels[z : z + 4], axis=0, keepdims=True)


def scattered(weights, panels, at_x, at_y, z):
    both = jnp.concatenate([at_y, at_y], axis=1)
    scaled = panels[z : z + 4] * weights
    high = scaled.astype(BF16).astype(F32)
    parts = [high, scaled - high]
    rows = [
        jnp.where(at_x[None], part[:, None, :], 0.0).reshape(4 * at_x.shape[0], -1).astype(BF16)
        for part in parts
    ]
    out = lax.dot_general(
        jnp.concatenate(rows, axis=1), both, NT, preferred_element_type=F32
    )
    return out.reshape(4, at_x.shape[0], at_y.shape[0])


def greet(devices):
    barrier = pltpu.get_barrier_semaphore()
    for device in devices:
        pl.semaphore_signal(barrier, inc=1, device_id=device, device_id_type=MESH)
    pl.semaphore_wait(barrier, len(devices))


def remote(source, target, sends, receives, device):
    return pltpu.make_async_remote_copy(
        src_ref=source,
        dst_ref=target,
        send_sem=sends,
        recv_sem=receives,
        device_id=device,
        device_id_type=MESH,
    )


def spread(
    members, grid_x, grid_y, fill, ready, use, background, line, sent, others, lines, got, mid,
    own_send, own_recv, relay_send, relay_recv, line_send, line_recv, pass_send, pass_recv,
    y_send, y_recv, x_send, x_recv, here,
):
    m, g, h = lax.axis_index("member"), lax.axis_index("gx"), lax.axis_index("gy")
    right = {"member": (m + 1) % members}
    left = {"member": (m + members - 1) % members}
    along_x = [{"gx": (g + d) % grid_x} for d in range(1, grid_x)]
    along_y = [{"gy": (h + d) % grid_y} for d in range(1, grid_y)]
    mate = {"gy": h + 1 - 2 * (h % 2)}
    greet([right, left] + along_x + along_y)

    chunks = own_send.shape[0] // 2
    size = background.shape[0] // chunks
    spans = [pl.ds(c * size, size) for c in range(chunks)]
    wide = lines.shape[1]
    part = wide // 2
    quads = line.shape[1] // wide
    start = pl.multiple_of((h % 2) * part, part)

    own = [
        remote(background.at[span], others.at[slot, span], own_send.at[2 * c + slot], own_recv.at[2 * c + slot], device)
        for c, span in enumerate(spans)
        for slot, device in ((0, right), (1, left))
    ]
    for copy in own:
        copy.start()
    pieces = []
    for d in range(1, grid_x):
        to = (g + d) % grid_x
        rows = pl.ds(pl.multiple_of((to % quads) * wide + start, part), part)
        pieces.append(
            remote(
                line.at[to // quads, rows],
                lines.at[g, pl.ds(start, part)],
                line_send.at[d - 1],
                line_recv.at[d - 1],
                along_x[d - 1],
            )
        )
    order = sorted(range(grid_x - 1), key=lambda k: min(k + 1, grid_x - 1 - k))
    early, late = order[: grid_x // 2], order[grid_x // 2 :]
    for k in early:
        pieces[k].start()
    mine_rows = pl.ds(pl.multiple_of((g % quads) * wide, wide), wide)
    level = pltpu.make_async_copy(line.at[g // quads, mine_rows], lines.at[g], here.at[1])
    level.start()

    fill()
    stations = [
        remote(sent.at[pl.ds((h + d) % grid_y * grid_x, grid_x)], mid.at[h], y_send.at[d - 1], y_recv.at[d - 1], along_y[d - 1])
        for d in range(1, grid_y)
    ]
    for copy in stations:
        copy.start()
    mine = pltpu.make_async_copy(sent.at[pl.ds(h * grid_x, grid_x)], mid.at[h], here.at[0])
    mine.start()
    mine.wait()
    for copy in stations:
        copy.wait_recv()
    second = [
        remote(mid.at[:, (g + d) % grid_x], got.at[pl.ds(g * grid_y, grid_y)], x_send.at[d - 1], x_recv.at[d - 1], along_x[d - 1])
        for d in range(1, grid_x)
    ]
    for copy in second:
        copy.start()
    last = pltpu.make_async_copy(mid.at[:, g], got.at[pl.ds(g * grid_y, grid_y)], here.at[2])
    last.start()
    for k in late:
        pieces[k].start()

    relay = []
    rows = background.shape[1] // 2
    for c, span in enumerate(spans):
        for slot, device in ((0, right), (1, left)):
            k = 2 * c + slot
            share = pl.ds(slot * rows, rows)
            own[k].wait_recv()
            relay.append(
                remote(
                    others.at[slot, span, share],
                    others.at[2, span, share],
                    relay_send.at[k],
                    relay_recv.at[k],
                    device,
                )
            )
            relay[k].start()

    last.wait()
    for copy in second:
        copy.wait_recv()
    ready()
    passed = []

    def hand_over(k):
        pieces[k].wait_recv()
        came = lines.at[(g + grid_x - 1 - k) % grid_x, pl.ds(start, part)]
        passed.append(remote(came, came, pass_send.at[k], pass_recv.at[k], mate))
        passed[-1].start()

    for k in early:
        hand_over(k)
    for c in range(chunks):
        relay[2 * c].wait_recv()
        relay[2 * c + 1].wait_recv()
        use(c)
    for k in late:
        hand_over(k)
    level.wait()
    return passed, own + relay + stations + second + pieces + passed


def unpack(slot_cap, got, panels, weights, cells):
    depth, tiles = panels.shape[0], got.shape[0]
    body = got[:, 0, :].T
    extra = got[:, 1, :].T
    for k in range(slot_cap):
        lanes = pl.ds(k * tiles, tiles)
        panels[:, lanes] = body[k * depth : (k + 1) * depth]
        weights[:, lanes] = extra[k : k + 1]
        cells[:, lanes] = extra[slot_cap + k : slot_cap + k + 1].astype(jnp.int32)


def steps_kernel(
    members, grid_x, grid_y, slot_cap,
    mixing, owner_row, panels_in, values, spots, background, line, scaling_in, kappa_in, prior, out,
    sent_slots, mid, got, others, mine_field, panels, weights, cells,
    whole, again, first, lines, scaling, kappa, x_rim, y_rim, x_low, x_high, y_low, y_high,
    own_send, own_recv, relay_send, relay_recv, line_send, line_recv, hand_send, hand_recv,
    y_send, y_recv, x_send, x_recv, there,
    far_send, far_recv, near_send, near_recv, pass_send, pass_recv, rim_send, rim_recv, here,
):
    depth, width_x, width_y = out.shape
    m = lax.axis_index("member")
    g, h = lax.axis_index("gx"), lax.axis_index("gy")
    flip = 2 - 4 * ((g // 2) % 2)
    turn = 1 - 2 * (g % 2)
    place, other = g % 4, (g + flip) % 4
    near, far = {"gx": g + turn}, {"gx": g + flip}
    up_y, down_y = {"gy": (h + 1) % grid_y}, {"gy": (h + grid_y - 1) % grid_y}
    fetched = [
        pltpu.make_async_copy(source, target, here.at[k])
        for k, (source, target) in enumerate(
            [(background, mine_field), (scaling_in, scaling), (kappa_in, kappa)]
        )
    ]
    for copy in fetched:
        copy.start()

    def fill():
        place_kernel(slot_cap, grid_y, owner_row, panels_in, values, spots, sent_slots)

    size = 4
    chunks = depth // size
    spans = [pl.ds(c * size, size) for c in range(chunks)]

    seen = []

    def ready():
        for copy in fetched:
            copy.wait()
        unpack(slot_cap, got, panels, weights, cells)
        seen.extend(masks(cells[...], width_x, width_y))

    def use_prior(c):
        z = c * size
        prior[z : z + size] = (
            mixing[m, m] * mine_field[z : z + size]
            + mixing[m, (m + members - 1) % members] * others[0, z : z + size]
            + mixing[m, (m + 1) % members] * others[1, z : z + size]
            + mixing[m, (m + 2) % members] * others[2, z : z + size]
        )
        weights[...] = weights[...] - project(prior, panels, *seen, z)

    passed, unsent = spread(
        members, grid_x, grid_y, fill, ready, use_prior, background, line, sent_slots, others, lines, got, mid,
        own_send, own_recv, relay_send, relay_recv, line_send, line_recv, hand_send, hand_recv,
        y_send, y_recv, x_send, x_recv, there,
    )
    at_x, at_y = seen

    def start_chunk(source, target, c, k):
        to_far = remote(source, target.at[place, spans[c]], far_send.at[k], far_recv.at[k], far)
        to_near = remote(source, target.at[place, spans[c]], near_send.at[k], near_recv.at[k], near)
        to_far.start()
        to_near.start()
        return to_far, to_near

    def solve(target, sent, base, use, done):
        handed = []

        def finish(c):
            sent[c][1].wait_recv()
            handed[c].wait_recv()
            for z in range(c * size, c * size + size):
                rows = jnp.concatenate([target[p, z] for p in range(4)], axis=0)
                left = jnp.concatenate(halves(lines[z]), axis=0)
                both = jnp.concatenate(halves(rows), axis=1)
                full = jnp.dot(left, both, preferred_element_type=F32)
                use(z, full[:width_x, :width_y] + (full[width_x:, :width_y] + full[:width_x, width_y:]))
            done(c)

        for c in range(chunks):
            sent[c][0].wait_recv()
            came = target.at[other, spans[c]]
            handed.append(remote(came, came, pass_send.at[base + c], pass_recv.at[base + c], near))
            handed[c].start()
            if c > 0:
                finish(c - 1)
        finish(chunks - 1)
        for c in range(chunks):
            sent[c][0].wait_send()
            sent[c][1].wait_send()
            handed[c].wait_send()

    lane = lax.broadcasted_iota(jnp.int32, (width_x, width_y), 1)
    row = lax.broadcasted_iota(jnp.int32, (width_x, width_y), 0)
    sent = []
    for c in range(chunks):
        whole[place, spans[c]] = scattered(weights[...], panels, at_x, at_y, c * size)
        sent.append(start_chunk(whole.at[place, spans[c]], whole, c, c))

    for copy in passed:
        copy.wait_recv()
    rims = [jnp.zeros((width_x, width_y), F32)]
    edges = []

    def use_first(z, level):
        c, j = z // size, z % size
        first[z] = level
        scaled = scaling[z] * level
        x_rim[c, j : j + 1] = scaled[:1]
        x_rim[c, size + j : size + j + 1] = scaled[width_x - 1 :]
        low = jnp.where(lane == j, scaled[:, :1], rims[0])
        rims[0] = jnp.where(lane == size + j, scaled[:, width_y - 1 :], low)

    def send_rims(c):
        y_rim[c] = rims[0]
        edges.append(
            [
                remote(source.at[c], target.at[c], rim_send.at[4 * c + k], rim_recv.at[4 * c + k], device)
                for k, (source, target, device) in enumerate(
                    [
                        (x_rim, x_low, {"gx": (g + 1) % grid_x}),
                        (x_rim, x_high, {"gx": (g + grid_x - 1) % grid_x}),
                        (y_rim, y_low, up_y),
                        (y_rim, y_high, down_y),
                    ]
                )
            ]
        )
        for copy in edges[c]:
            copy.start()
        weights[...] = weights[...] - project(first, panels, at_x, at_y, c * size)

    solve(whole, sent, 0, use_first, send_rims)
    left = weights[...]
    sent = []
    for c in range(chunks):
        summed = scattered(left, panels, at_x, at_y, c * size)
        for copy in edges[c]:
            copy.wait()
        low_x = jnp.where(g > 0, x_low[c], 0.0)
        high_x = jnp.where(g < grid_x - 1, x_high[c], 0.0)
        low_y = jnp.where(h > 0, y_low[c], 0.0)
        high_y = jnp.where(h < grid_y - 1, y_high[c], 0.0)
        for k in range(c * size, c * size + size):
            j = k - c * size
            here_u = scaling[k] * first[k]
            beside = jnp.where(row == 0, low_x[size + j : size + j + 1], pltpu.roll(here_u, 1, 0))
            beside = beside + jnp.where(
                row == width_x - 1, high_x[j : j + 1], pltpu.roll(here_u, width_x - 1, 0)
            )
            beside = beside + jnp.where(
                lane == 0, low_y[:, size + j : size + j + 1], pltpu.roll(here_u, 1, 1)
            )
            beside = beside + jnp.where(
                lane == width_y - 1, high_y[:, j : j + 1], pltpu.roll(here_u, width_y - 1, 1)
            )
            if k > 0:
                beside = beside + scaling[k - 1] * first[k - 1]
            if k < depth - 1:
                beside = beside + scaling[k + 1] * first[k + 1]
            again[place, k] = summed[k - c * size] - (
                kappa[k] * first[k] + scaling[k] * (6.0 * here_u - beside)
            )
        sent.append(start_chunk(again.at[place, spans[c]], again, c, chunks + c))

    def use_second(z, level):
        out[z] = first[z] + level

    solve(again, sent, chunks, use_second, lambda c: None)
    for copy in unsent:
        copy.wait_send()


def shape(*dims, dtype=F32):
    return jax.ShapeDtypeStruct(dims, dtype)


def dma(count):
    return pltpu.SemaphoreType.DMA((count,))


def shards(background, mixing, kappa_sq, scaling, line_inverse, panels, values, targets, spots):
    depth, width_x, width_y = kappa_sq.shape
    members = lax.axis_size("member")
    grid_x, grid_y = lax.axis_size("gx"), lax.axis_size("gy")
    tiles = grid_x * grid_y
    count = spots.shape[0]
    slot_cap = max(2, 2 * count // tiles)
    field = shape(depth, width_x, width_y)
    line = line_inverse.shape[2]
    background, line_inverse = background[0], line_inverse[0]
    slots = tiles * slot_cap
    packet = pltpu.VMEM((tiles, 2, slot_cap * depth), F32)
    block = pltpu.VMEM((depth, width_x, width_y), F32)
    gathered = pltpu.VMEM((4, depth, width_x, width_y), F32)
    x_edge = pltpu.VMEM((4, depth // 2, width_y), F32)
    y_edge = pltpu.VMEM((4, width_x, width_y), F32)
    far_x, far_y = grid_x - 1, grid_y - 1
    prior, second = pl.pallas_call(
        functools.partial(steps_kernel, members, grid_x, grid_y, slot_cap),
        out_shape=(field, field),
        in_specs=[pl.BlockSpec(memory_space=pltpu.SMEM)] + [VMEM] * 4 + [ANY] * 4,
        out_specs=(VMEM, VMEM),
        scratch_shapes=[
            packet,
            pltpu.VMEM((grid_y, grid_x, 2, slot_cap * depth), F32),
            packet,
            pltpu.VMEM((members - 1, depth, width_x, width_y), F32),
            block,
            pltpu.VMEM((depth, slots), F32),
            pltpu.VMEM((1, slots), F32),
            pltpu.VMEM((1, slots), jnp.int32),
            gathered, gathered, block, pltpu.VMEM((depth, width_x, line), F32), block, block,
            x_edge, y_edge, x_edge, x_edge, y_edge, y_edge,
            dma(8), dma(8), dma(8), dma(8), dma(far_x), dma(far_x), dma(far_x), dma(far_x),
            dma(far_y), dma(far_y), dma(far_x), dma(far_x), dma(3),
            dma(8), dma(8), dma(8), dma(8), dma(8), dma(8), dma(16), dma(16), dma(3),
        ],
        compiler_params=pltpu.CompilerParams(collective_id=0, has_side_effects=True),
    )(
        mixing, targets.reshape(1, count), panels, values, spots.reshape(1, count),
        background, line_inverse, scaling, kappa_sq,
    )
    return (prior + second)[None]


def solution(mesh):
    return jax.shard_map(
        shards,
        mesh=mesh,
        in_specs=(
            P("member", None, "gx", "gy"),
            P(),
            P(None, "gx", "gy"),
            P(None, "gx", "gy"),
            P("gx", None, None, None),
            P(None, ("gx", "gy")),
            P("member", ("gx", "gy")),
            P(("gx", "gy"), None),
            P(("gx", "gy")),
        ),
        out_specs=P("member", None, "gx", "gy"),
        check_vma=False,
    )
```
